32 devices in a mesh: groups: 2 (over y), ta: 4 (over z), gz: 2 (over x), rep: 2 (over core).
Axes of the slice: x: 2, y: 2, z: 4, core: 2. Of those that a mesh axis runs over, the one named last changes fastest.
Arguments:
- gauge_links: float32 [4, 4, 4, 2, 3, 3, 4, 256], P(('groups', 'rep'), 'ta', 'gz'), parts along dimension 0, may hold values from -1 to 1, as said below
- input_field: float32 [4, 4, 4, 2, 3, 3, 4, 256], P(('groups', 'rep'), 'ta', 'gz'), parts along dimension 0, may hold values from -6 to 6
- conv_weights: float32 [4, 4, 9], replicated, may hold values from -1 to 1
- loss_weight: float32 [4, 4, 4, 256], P(('groups', 'rep'), 'ta', 'gz'), parts along dimension 0, may hold values from 0.005 to 18, as said below
Outputs:
- output_field: float32 [4, 4, 4, 2, 3, 3, 4, 256], P(('groups', 'rep'), 'ta', 'gz'), parts along dimension 0
- field_grad: float32 [4, 4, 4, 2, 3, 3, 4, 256], P(('groups', 'rep'), 'ta', 'gz'), parts along dimension 0
- weight_grad: float32 [8, 4, 9], P('groups'), parts along dimension 0
The draws below stay inside these ranges and needn't reach their ends.
There are 2 independent parts, one for each index of `groups`. The reference program is written for one: setup_inputs(seed, part) draws one part's arguments, and reference() takes and returns one part's arrays. A program takes and returns all parts, laid end to end along the dimension named above; an argument that names none is the same for every part. Nothing has to cross between parts.
Inputs may be any that keep to these rules, and one draw needn't show every extreme that they name: `gauge_links`: every link is a special unitary 3x3 matrix. `loss_weight`: positive.
All inputs are finite; a program needn't handle non-finite values.
Results may differ from the reference program's by a relative error of at most 0.00014.
Values sent between devices are 32-bit elements; how exact they have to be, the bound alone decides.
No kernel may reach another device: no remote copies, remote signals or barrier semaphores. Data moves between devices by JAX's collectives and lax.ppermute only.
A program may use at most 128 MiB of HBM per device.

```python
import math
import jax
import jax.numpy as jnp
from jax import lax

NCH = 4
TERMS = 9
LY = 16
LX = 16
CONFS = 2
T_EXT = 4
Z_EXT = 4
SITES = 8192


def draw_matmul(left_matrix, right_matrix):
    return jnp.sum(left_matrix[:, :, None] * right_matrix[None, :, :], axis=1)


def draw_product(left_matrix, right_matrix):
    real_part = draw_matmul(left_matrix[0], right_matrix[0]) - draw_matmul(left_matrix[1], right_matrix[1])
    imag_part = draw_matmul(left_matrix[0], right_matrix[1]) + draw_matmul(left_matrix[1], right_matrix[0])
    return jnp.stack([real_part, imag_part])


def stack_rows(real_rows, imag_rows):
    real_part = jnp.stack([jnp.stack(matrix_row) for matrix_row in real_rows])
    imag_part = jnp.stack([jnp.stack(matrix_row) for matrix_row in imag_rows])
    return jnp.stack([real_part, imag_part])


def embed_pair(first_index, second_index, theta, phase_one, phase_two):
    unit_part = jnp.ones_like(theta)
    null_part = jnp.zeros_like(theta)
    real_rows = [[unit_part if row_index == col_index else null_part for col_index in range(3)] for row_index in range(3)]
    imag_rows = [[null_part for col_index in range(3)] for row_index in range(3)]
    cosine = jnp.cos(theta)
    sine_value = jnp.sin(theta)
    real_rows[first_index][first_index] = cosine * jnp.cos(phase_one)
    imag_rows[first_index][first_index] = cosine * jnp.sin(phase_one)
    real_rows[second_index][second_index] = cosine * jnp.cos(phase_one)
    imag_rows[second_index][second_index] = -cosine * jnp.sin(phase_one)
    real_rows[second_index][first_index] = sine_value * jnp.cos(phase_two)
    imag_rows[second_index][first_index] = sine_value * jnp.sin(phase_two)
    real_rows[first_index][second_index] = -sine_value * jnp.cos(phase_two)
    imag_rows[first_index][second_index] = sine_value * jnp.sin(phase_two)
    return stack_rows(real_rows, imag_rows)


def draw_gauge_links(key, part):
    site_shape = (CONFS, T_EXT, Z_EXT, 4, LY * LX)
    angles = jax.random.uniform(key, (11,) + site_shape, jnp.float32, -math.pi, math.pi)
    null_part = jnp.zeros(site_shape, jnp.float32)
    phase_three = -angles[0] - angles[1]
    real_rows = [[null_part for col_index in range(3)] for row_index in range(3)]
    imag_rows = [[null_part for col_index in range(3)] for row_index in range(3)]
    real_rows[0][0] = jnp.cos(angles[0])
    imag_rows[0][0] = jnp.sin(angles[0])
    real_rows[1][1] = jnp.cos(angles[1])
    imag_rows[1][1] = jnp.sin(angles[1])
    real_rows[2][2] = jnp.cos(phase_three)
    imag_rows[2][2] = jnp.sin(phase_three)
    result = stack_rows(real_rows, imag_rows)
    result = draw_product(result, embed_pair(0, 1, angles[2], angles[3], angles[4]))
    result = draw_product(result, embed_pair(1, 2, angles[5], angles[6], angles[7]))
    result = draw_product(result, embed_pair(0, 2, angles[8], angles[9], angles[10]))
    return jnp.transpose(result, (3, 4, 5, 0, 1, 2, 6, 7))


def ramp_values(index_values, length, ramp_low):
    return ramp_low + index_values / (length - 1)


def draw_loss_weight(key, part):
    full_shape = (CONFS, T_EXT, Z_EXT, LY * LX)
    config_index = jnp.arange(CONFS).astype(jnp.float32).reshape(CONFS, 1, 1, 1)
    time_index = jnp.arange(T_EXT).astype(jnp.float32).reshape(1, T_EXT, 1, 1)
    depth_index = jnp.arange(Z_EXT).astype(jnp.float32).reshape(1, 1, Z_EXT, 1)
    ramp_low = 0.5
    roughness = jax.random.uniform(key, full_shape, jnp.float32, 0.7, 1.4)
    ramps = ramp_values(config_index, CONFS, ramp_low) * ramp_values(time_index, T_EXT, ramp_low) * ramp_values(depth_index, Z_EXT, ramp_low)
    return ramps * roughness


def level_of(rng, dims, shards, least, high):
    gain = 1.0
    for position, blocks in shards:
        steps = jax.random.uniform(jax.random.fold_in(jax.random.fold_in(rng, 6), position), (blocks,), jnp.float32, least / len(shards), high / len(shards))
        gain = gain * jnp.repeat(jnp.exp(steps), dims[position] // blocks).reshape((-1,) + (1,) * (len(dims) - 1 - position))
    return gain


def bell_draw(own_key, shape, width, most, pieces=(), kind=jnp.bfloat16):
    values = width * jax.random.normal(own_key, shape, jnp.float32)
    if pieces:
        values = values * level_of(own_key, shape, pieces, -0.22, 0.18)
    return jnp.clip(values, -most, most).astype(kind)


def setup_inputs(seed: int = 0, part: int = 0) -> dict:
    key_of = jax.random.split(jax.random.key(seed), 5)
    part_keys = jax.random.split(jax.random.fold_in(key_of[4], part), 5)
    gauge_links = draw_gauge_links(jax.random.fold_in(jax.random.fold_in(key_of[4], part), 71), part)
    input_field = bell_draw(part_keys[1], (CONFS, T_EXT, Z_EXT, 2, 3, 3, NCH, LY * LX), 1.0, 6.0, ((0, 2), (1, 4), (2, 2)), jnp.float32)
    conv_weights = bell_draw(key_of[2], (NCH, NCH, TERMS), (TERMS * NCH) ** -0.5, 1.0, (), jnp.float32)
    loss_weight = draw_loss_weight(jax.random.fold_in(jax.random.fold_in(key_of[4], part), 71), part)
    return {"gauge_links": gauge_links, "input_field": input_field, "conv_weights": conv_weights, "loss_weight": loss_weight}


HIGHEST = lax.Precision.HIGHEST


def element(matrix, part_index, row_index, col_index):
    return matrix[:, :, :, part_index, row_index, col_index]


def complex_product(left_matrix, right_matrix):
    real_rows = []
    imag_rows = []
    for row_index in range(3):
        real_line = []
        imag_line = []
        for col_index in range(3):
            real_sum = 0.0
            imag_sum = 0.0
            for inner in range(3):
                left_real = element(left_matrix, 0, row_index, inner)
                left_imag = element(left_matrix, 1, row_index, inner)
                right_real = element(right_matrix, 0, inner, col_index)
                right_imag = element(right_matrix, 1, inner, col_index)
                real_sum = real_sum + left_real * right_real - left_imag * right_imag
                imag_sum = imag_sum + left_real * right_imag + left_imag * right_real
            real_line.append(real_sum)
            imag_line.append(imag_sum)
        real_rows.append(jnp.stack(real_line, axis=3))
        imag_rows.append(jnp.stack(imag_line, axis=3))
    return jnp.stack([jnp.stack(real_rows, axis=3), jnp.stack(imag_rows, axis=3)], axis=3)


def conjugate_transpose(matrix):
    real_part = jnp.swapaxes(matrix[:, :, :, 0], 3, 4)
    imag_part = -jnp.swapaxes(matrix[:, :, :, 1], 3, 4)
    return jnp.stack([real_part, imag_part], axis=3)


def rolled(values, direction, offset):
    if direction == 0:
        return jnp.roll(values, -offset, axis=1)
    if direction == 1:
        return jnp.roll(values, -offset, axis=2)
    full_shape = values.shape
    plane_grid = values.reshape(full_shape[:-1] + (LY, LX))
    plane_grid = jnp.roll(plane_grid, -offset, axis=-2 if direction == 2 else -1)
    return plane_grid.reshape(full_shape)


def mix(weights, values):
    return jnp.einsum('ij,ctzpabjs->ctzpabis', weights, values, precision=HIGHEST)


def reference(gauge_links, input_field, conv_weights, loss_weight):
    hop_terms = [input_field]
    for direction in range(4):
        link_dir = gauge_links[:, :, :, :, :, :, direction:direction + 1]
        carried = complex_product(complex_product(conjugate_transpose(link_dir), input_field), link_dir)
        forward_hop = complex_product(complex_product(link_dir, rolled(input_field, direction, 1)), conjugate_transpose(link_dir))
        hop_terms.append(forward_hop)
        hop_terms.append(rolled(carried, direction, -1))
    output_field = mix(conv_weights[:, :, 0], hop_terms[0])
    for term_index in range(1, len(hop_terms)):
        output_field = output_field + mix(conv_weights[:, :, term_index], hop_terms[term_index])
    cotangent = loss_weight[:, :, :, None, None, None, None, :] * output_field
    weight_grad = jnp.stack([jnp.einsum('ctzpabis,ctzpabjs->ij', cotangent, term, precision=HIGHEST) for term in hop_terms], axis=-1) / SITES
    mixed_cot = [mix(conv_weights[:, :, term_index].T, cotangent) for term_index in range(TERMS)]
    accumulated = mixed_cot[0]
    for direction in range(4):
        link_dir = gauge_links[:, :, :, :, :, :, direction:direction + 1]
        pulled = complex_product(complex_product(conjugate_transpose(link_dir), mixed_cot[1 + 2 * direction]), link_dir)
        accumulated = accumulated + rolled(pulled, direction, -1)
        accumulated = accumulated + complex_product(complex_product(link_dir, rolled(mixed_cot[2 + 2 * direction], direction, 1)), conjugate_transpose(link_dir))
    return output_field, accumulated, weight_grad
```

```python
import jax
import jax.numpy as jnp
import numpy as np
from jax import lax
from jax.experimental import pallas as pl
from jax.experimental.pallas import tpu as pltpu
from jax.sharding import PartitionSpec as P

PLANES = 2
NCH = 4
TERMS = 9
COMPS = 18
HALF = 2
ROWS = HALF * NCH
LANES = 128
LX = 16
FIELD = (PLANES, COMPS, ROWS, LANES)
F32 = jnp.float32


def to_rows(block):
    planes = block.size // (COMPS * ROWS * LANES)
    split = block.reshape(planes, COMPS, NCH, HALF, LANES)
    return split.transpose(0, 1, 3, 2, 4).reshape(planes, COMPS, ROWS, LANES)


def from_rows(rows, shape):
    split = rows.reshape(PLANES, COMPS, HALF, NCH, LANES)
    return split.transpose(0, 1, 3, 2, 4).reshape(shape)


def sublane_index():
    return lax.broadcasted_iota(jnp.int32, (ROWS, LANES), 0)


def lane_index():
    return lax.broadcasted_iota(jnp.int32, (ROWS, LANES), 1)


def pick_rows(value, index):
    return jnp.take_along_axis(value, index, axis=0, mode="promise_in_bounds")


def as_matrix(items):
    return [[[items[p * 9 + r * 3 + c] for c in range(3)] for r in range(3)] for p in range(2)]


def as_items(matrix):
    return [matrix[p][r][c] for p in range(2) for r in range(3) for c in range(3)]


def total(items):
    result = items[0]
    for item in items[1:]:
        result = result + item
    return result


def product(left, right):
    (lr, li), (rr, ri) = left, right
    out = [[], []]
    for r in range(3):
        out[0].append(
            [
                total([lr[r][k] * rr[k][c] for k in range(3)])
                - total([li[r][k] * ri[k][c] for k in range(3)])
                for c in range(3)
            ]
        )
        out[1].append(
            [
                total([lr[r][k] * ri[k][c] for k in range(3)])
                + total([li[r][k] * rr[k][c] for k in range(3)])
                for c in range(3)
            ]
        )
    return out


def product_left_dagger(left, right):
    (lr, li), (rr, ri) = left, right
    out = [[], []]
    for r in range(3):
        out[0].append(
            [
                total([lr[k][r] * rr[k][c] for k in range(3)])
                + total([li[k][r] * ri[k][c] for k in range(3)])
                for c in range(3)
            ]
        )
        out[1].append(
            [
                total([lr[k][r] * ri[k][c] for k in range(3)])
                - total([li[k][r] * rr[k][c] for k in range(3)])
                for c in range(3)
            ]
        )
    return out


def product_right_dagger(left, right):
    (lr, li), (rr, ri) = left, right
    out = [[], []]
    for r in range(3):
        out[0].append(
            [
                total([lr[r][k] * rr[c][k] for k in range(3)])
                + total([li[r][k] * ri[c][k] for k in range(3)])
                for c in range(3)
            ]
        )
        out[1].append(
            [
                total([li[r][k] * rr[c][k] for k in range(3)])
                - total([lr[r][k] * ri[c][k] for k in range(3)])
                for c in range(3)
            ]
        )
    return out


def hop_forward(link, items):
    matrix = as_matrix(items)
    return as_items(product_right_dagger(product(link, matrix), link))


def hop_backward(link, items):
    matrix = as_matrix(items)
    return as_items(product(product_left_dagger(link, matrix), link))


def load_items(ref, plane):
    return [ref[plane, comp] for comp in range(COMPS)]


def load_link(ref, plane, direction):
    index = (sublane_index() & 4) + direction
    return as_matrix([pick_rows(ref[plane, comp], index) for comp in range(COMPS)])


def load_sent_link(ref, plane):
    base = lax.shift_right_logical(sublane_index(), 2)
    items = []
    for comp in range(COMPS):
        row = (plane * COMPS + comp) * HALF
        start = row // ROWS * ROWS
        items.append(pick_rows(ref[start : start + ROWS, :], base + (row - start)))
    return as_matrix(items)


def step_plane(value, direction, offset):
    lane = lane_index()
    if direction == 3:
        inner = lane & (LX - 1)
        if offset > 0:
            return jnp.where(
                inner == LX - 1,
                pltpu.roll(value, LX - 1, axis=1),
                pltpu.roll(value, LANES - 1, axis=1),
            )
        return jnp.where(
            inner == 0,
            pltpu.roll(value, LANES - LX + 1, axis=1),
            pltpu.roll(value, 1, axis=1),
        )
    if offset > 0:
        moved = pltpu.roll(value, LANES - LX, axis=1)
        return jnp.where(lane >= LANES - LX, pltpu.roll(moved, NCH, axis=0), moved)
    moved = pltpu.roll(value, LX, axis=1)
    return jnp.where(lane < LX, pltpu.roll(moved, NCH, axis=0), moved)


def step_items(items, direction, offset):
    return [step_plane(item, direction, offset) for item in items]


def turned(value):
    sub = sublane_index()
    return [value] + [pick_rows(value, (sub & 4) | ((sub + d) & 3)) for d in range(1, NCH)]


def weight_rows(ref, base, term):
    first = base + term * NCH
    return [
        jnp.broadcast_to(ref[:, first + d : first + d + 1], (ROWS, LANES)) for d in range(NCH)
    ]


def mixed_item(weights, turns):
    return total([weights[d] * turns[d] for d in range(NCH)])


def mixed_items(weights, items):
    return [mixed_item(weights, turned(item)) for item in items]


FORWARD = 0
BACKWARD = TERMS * NCH


def near_forward(field, links, weights, partial, terms):
    for plane in range(PLANES):
        items = load_items(field, plane)
        sums = mixed_items(weight_rows(weights, FORWARD, 0), items)

        def add(term, hop, slot):
            mixed = mixed_items(weight_rows(weights, FORWARD, term), hop)
            for comp in range(COMPS):
                terms[slot, plane, comp] = hop[comp]
                sums[comp] = sums[comp] + mixed[comp]

        for direction in (2, 3):
            link = load_link(links, plane, direction)
            slot = 2 * (direction - 2)
            add(
                2 * direction + 1,
                hop_forward(link, step_items(items, direction, 1)),
                slot,
            )
            add(
                2 * direction + 2,
                step_items(hop_backward(link, items), direction, -1),
                slot + 1,
            )
        link = load_link(links, 0, 1)
        other = load_items(field, 1 - plane)
        if plane == 0:
            add(3, hop_forward(link, other), 4)
        else:
            add(4, hop_backward(link, other), 4)
        for comp in range(COMPS):
            partial[plane, comp] = sums[comp]


def far_forward(
    links, weights, loss, partial, t_next, t_prev, t_link, z_field, z_link, out, cot, terms
):
    for plane in range(PLANES):
        sums = load_items(partial, plane)

        def add(term, hop, slot):
            mixed = mixed_items(weight_rows(weights, FORWARD, term), hop)
            for comp in range(COMPS):
                terms[slot, plane, comp] = hop[comp]
                sums[comp] = sums[comp] + mixed[comp]

        if plane == 0:
            add(4, hop_backward(load_sent_link(z_link, 0), load_items(z_field, 1)), 2)
        else:
            add(3, hop_forward(load_link(links, 1, 1), load_items(z_field, 0)), 2)
        add(1, hop_forward(load_link(links, plane, 0), load_items(t_next, plane)), 0)
        add(2, hop_backward(load_sent_link(t_link, plane), load_items(t_prev, plane)), 1)
        row = loss[plane : plane + 1, :]
        scale = jnp.where(
            sublane_index() < NCH,
            jnp.broadcast_to(row[:, :LANES], (ROWS, LANES)),
            jnp.broadcast_to(row[:, LANES:], (ROWS, LANES)),
        )
        for comp in range(COMPS):
            out[plane, comp] = sums[comp]
            cot[plane, comp] = scale * sums[comp]


def term_item(field, near, far, term, plane, comp):
    if term == 0:
        return field[plane, comp]
    if term >= 5:
        return near[term - 5, plane, comp]
    if term <= 2:
        return far[term - 1, plane, comp]
    if (term == 3) == (plane == 0):
        return near[4, plane, comp]
    return far[2, plane, comp]


def weight_sums(field, cot, near, far, sums, spread):
    sub = sublane_index()
    lane = lane_index()
    for channel in range(NCH):
        index = (sub & 4) + channel
        for plane in range(PLANES):
            for comp in range(COMPS):
                spread[channel, plane, comp] = pick_rows(cot[plane, comp], index)
    rows = [jnp.zeros((ROWS, LANES), F32) for _ in range(NCH)]
    for term in range(TERMS):
        parts = [None] * NCH
        for plane in range(PLANES):
            for comp in range(COMPS):
                value = term_item(field, near, far, term, plane, comp)
                for channel in range(NCH):
                    piece = spread[channel, plane, comp] * value
                    parts[channel] = piece if parts[channel] is None else parts[channel] + piece
        for channel in range(NCH):
            summed = jnp.sum(parts[channel], axis=1, keepdims=True)
            rows[channel] = jnp.where(lane == term, summed, rows[channel])
    for channel in range(NCH):
        both = rows[channel] + pltpu.roll(rows[channel], NCH, axis=0)
        sums[channel] = both[:NCH, :TERMS]


def near_backward(field, links, weights, cot, near, far, sums, partial, spread):
    weight_sums(field, cot, near, far, sums, spread)
    for plane in range(PLANES):
        turns = [turned(cot[plane, comp]) for comp in range(COMPS)]

        def mixed(term):
            rows = weight_rows(weights, BACKWARD, term)
            return [mixed_item(rows, turn) for turn in turns]

        grads = mixed(0)

        def add(hop):
            for comp in range(COMPS):
                grads[comp] = grads[comp] + hop[comp]

        for direction in (2, 3):
            link = load_link(links, plane, direction)
            pulled = hop_backward(link, mixed(2 * direction + 1))
            add(step_items(pulled, direction, -1))
            add(hop_forward(link, step_items(mixed(2 * direction + 2), direction, 1)))
        for comp in range(COMPS):
            partial[plane, comp] = grads[comp]
    link = load_link(links, 0, 1)
    hop = hop_forward(link, mixed_items(weight_rows(weights, BACKWARD, 4), load_items(cot, 1)))
    for comp in range(COMPS):
        partial[0, comp] = partial[0, comp] + hop[comp]
    hop = hop_backward(link, mixed_items(weight_rows(weights, BACKWARD, 3), load_items(cot, 0)))
    for comp in range(COMPS):
        partial[1, comp] = partial[1, comp] + hop[comp]


def far_backward(links, weights, partial, t_next, t_prev, t_link, z_cot, z_link, grad):
    for plane in range(PLANES):
        grads = load_items(partial, plane)

        def mixed(term, ref, source):
            return mixed_items(weight_rows(weights, BACKWARD, term), load_items(ref, source))

        def add(hop):
            for comp in range(COMPS):
                grads[comp] = grads[comp] + hop[comp]

        if plane == 0:
            add(hop_backward(load_sent_link(z_link, 0), mixed(3, z_cot, 1)))
        else:
            add(hop_forward(load_link(links, 1, 1), mixed(4, z_cot, 0)))
        add(hop_forward(load_link(links, plane, 0), mixed(2, t_next, plane)))
        add(hop_backward(load_sent_link(t_link, plane), mixed(1, t_prev, plane)))
        for comp in range(COMPS):
            grad[plane, comp] = grads[comp]


def run(kernel, shapes, *operands, scratch=()):
    outs = [jax.ShapeDtypeStruct(shape, F32) for shape in shapes]
    return pl.pallas_call(
        kernel,
        out_shape=outs,
        scratch_shapes=list(scratch),
        compiler_params=pltpu.CompilerParams(vmem_limit_bytes=32 * 2**20),
    )(*operands)


def shifted(value, axis, offset):
    count = lax.axis_size(axis)
    return lax.ppermute(value, axis, [(i, (i + offset) % count) for i in range(count)])


def z_planes(block):
    if lax.axis_size("gz") == 2:
        return shifted(block, "gz", 1)
    return jnp.concatenate([shifted(block[:1], "gz", -1), shifted(block[1:], "gz", 1)], axis=0)


def summed_over(value, axes):
    for axis in axes:
        count = lax.axis_size(axis)
        if count & (count - 1):
            value = lax.psum(value, axis)
            continue
        step = 1
        while step < count:
            value = value + lax.ppermute(value, axis, [(i, i ^ step) for i in range(count)])
            step *= 2
    return value


def weight_table(conv_weights):
    out_index, in_index, turn = np.indices((NCH, NCH, NCH))
    forward_pick = ((out_index + turn) % NCH == in_index).astype(np.float32)
    backward_pick = ((in_index + turn) % NCH == out_index).astype(np.float32)
    wide = conv_weights[:, :, :, None]
    forward = jnp.sum(wide * forward_pick[:, :, None, :], axis=1)
    backward = jnp.sum(wide * backward_pick[:, :, None, :], axis=0)
    table = jnp.concatenate(
        [forward.reshape(NCH, TERMS * NCH), backward.reshape(NCH, TERMS * NCH)], axis=1
    )
    return jnp.concatenate([table, table], axis=0)


def local(gauge_links, input_field, conv_weights, loss_weight):
    shape = input_field.shape
    field = to_rows(input_field)
    links = to_rows(gauge_links)
    t_link = gauge_links[:, :, :, :, :, :, 0].reshape(PLANES * COMPS * HALF, LANES)
    z_link = gauge_links[:, :, 1, :, :, :, 1].reshape(COMPS * HALF, LANES)
    z_field = z_planes(field)
    t_next = shifted(field, "ta", -1)
    t_prev = shifted(field, "ta", 1)
    z_link = shifted(z_link, "gz", 1)
    t_link = shifted(t_link, "ta", 1)
    weights = weight_table(conv_weights)
    loss = loss_weight.reshape(PLANES, HALF * LANES)
    partial, near = run(near_forward, (FIELD, (5,) + FIELD), field, links, weights)
    out, cot, far = run(
        far_forward,
        (FIELD, FIELD, (3,) + FIELD),
        links,
        weights,
        loss,
        partial,
        t_next,
        t_prev,
        t_link,
        z_field,
        z_link,
    )
    z_cot = z_planes(cot)
    t_next_cot = shifted(cot, "ta", -1)
    t_prev_cot = shifted(cot, "ta", 1)
    sums, grad_partial = run(
        near_backward,
        ((NCH, NCH, TERMS), FIELD),
        field,
        links,
        weights,
        cot,
        near,
        far,
        scratch=[pltpu.VMEM((NCH,) + FIELD, F32)],
    )
    sums = summed_over(sums, ("rep", "gz", "ta"))
    count = loss_weight.size
    for axis in ("ta", "gz", "rep"):
        count = count * lax.axis_size(axis)
    weight_grad = sums / count
    (grad,) = run(
        far_backward,
        (FIELD,),
        links,
        weights,
        grad_partial,
        t_next_cot,
        t_prev_cot,
        t_link,
        z_cot,
        z_link,
    )
    return from_rows(out, shape), from_rows(grad, shape), weight_grad


def solution(mesh):
    split = P(("groups", "rep"), "ta", "gz", None, None, None, None, None)
    return jax.shard_map(
        local,
        mesh=mesh,
        in_specs=(split, split, P(), P(("groups", "rep"), "ta", "gz", None)),
        out_specs=(split, split, P("groups", None, None)),
        check_vma=False,
    )
```

```python
import functools

import jax
import jax.numpy as jnp
import numpy as np
from jax import lax
from jax.experimental import pallas as pl
from jax.experimental.pallas import tpu as pltpu
from jax.sharding import PartitionSpec as P

PLANES = 2
NCH = 4
TERMS = 9
COMPS = 18
HALF = 2
ROWS = HALF * NCH
LANES = 128
LX = 16
FIELD = (PLANES, COMPS, ROWS, LANES)
MESSAGE = (PLANES * COMPS + 1, ROWS, LANES)
TILE = (ROWS, LANES)
F32 = jnp.float32


def to_rows(block):
    planes = block.size // (COMPS * ROWS * LANES)
    split = block.reshape(planes, COMPS, NCH, HALF, LANES)
    return split.transpose(0, 1, 3, 2, 4).reshape(planes, COMPS, ROWS, LANES)


def from_rows(rows, shape):
    split = rows.reshape(PLANES, COMPS, HALF, NCH, LANES)
    return split.transpose(0, 1, 3, 2, 4).reshape(shape)


def sublane_index():
    return lax.broadcasted_iota(jnp.int32, (ROWS, LANES), 0)


def lane_index():
    return lax.broadcasted_iota(jnp.int32, (ROWS, LANES), 1)


def pick_rows(value, index):
    return jnp.take_along_axis(value, index, axis=0, mode="promise_in_bounds")


def as_matrix(items):
    return [[[items[p * 9 + r * 3 + c] for c in range(3)] for r in range(3)] for p in range(2)]


def as_items(matrix):
    return [matrix[p][r][c] for p in range(2) for r in range(3) for c in range(3)]


def total(items):
    result = items[0]
    for item in items[1:]:
        result = result + item
    return result


def product(left, right):
    (lr, li), (rr, ri) = left, right
    out = [[], []]
    for r in range(3):
        out[0].append(
            [
                total([lr[r][k] * rr[k][c] for k in range(3)])
                - total([li[r][k] * ri[k][c] for k in range(3)])
                for c in range(3)
            ]
        )
        out[1].append(
            [
                total([lr[r][k] * ri[k][c] for k in range(3)])
                + total([li[r][k] * rr[k][c] for k in range(3)])
                for c in range(3)
            ]
        )
    return out


def product_left_dagger(left, right):
    (lr, li), (rr, ri) = left, right
    out = [[], []]
    for r in range(3):
        out[0].append(
            [
                total([lr[k][r] * rr[k][c] for k in range(3)])
                + total([li[k][r] * ri[k][c] for k in range(3)])
                for c in range(3)
            ]
        )
        out[1].append(
            [
                total([lr[k][r] * ri[k][c] for k in range(3)])
                - total([li[k][r] * rr[k][c] for k in range(3)])
                for c in range(3)
            ]
        )
    return out


def product_right_dagger(left, right):
    (lr, li), (rr, ri) = left, right
    out = [[], []]
    for r in range(3):
        out[0].append(
            [
                total([lr[r][k] * rr[c][k] for k in range(3)])
                + total([li[r][k] * ri[c][k] for k in range(3)])
                for c in range(3)
            ]
        )
        out[1].append(
            [
                total([li[r][k] * rr[c][k] for k in range(3)])
                - total([lr[r][k] * ri[c][k] for k in range(3)])
                for c in range(3)
            ]
        )
    return out


def hop_forward(link, items):
    matrix = as_matrix(items)
    return as_items(product_right_dagger(product(link, matrix), link))


def hop_backward(link, items):
    matrix = as_matrix(items)
    return as_items(product(product_left_dagger(link, matrix), link))


def load_items(ref, plane):
    return [ref[plane, comp] for comp in range(COMPS)]


def load_link(ref, plane, direction):
    index = (sublane_index() & 4) + direction
    return as_matrix([pick_rows(ref[plane, comp], index) for comp in range(COMPS)])


def step_plane(value, direction, offset):
    lane = lane_index()
    if direction == 3:
        inner = lane & (LX - 1)
        if offset > 0:
            return jnp.where(
                inner == LX - 1,
                pltpu.roll(value, LX - 1, axis=1),
                pltpu.roll(value, LANES - 1, axis=1),
            )
        return jnp.where(
            inner == 0,
            pltpu.roll(value, LANES - LX + 1, axis=1),
            pltpu.roll(value, 1, axis=1),
        )
    if offset > 0:
        moved = pltpu.roll(value, LANES - LX, axis=1)
        return jnp.where(lane >= LANES - LX, pltpu.roll(moved, NCH, axis=0), moved)
    moved = pltpu.roll(value, LX, axis=1)
    return jnp.where(lane < LX, pltpu.roll(moved, NCH, axis=0), moved)


def step_items(items, direction, offset):
    return [step_plane(item, direction, offset) for item in items]


def turned(value):
    sub = sublane_index()
    return [value] + [pick_rows(value, (sub & 4) | ((sub + d) & 3)) for d in range(1, NCH)]


def weight_rows(ref, base, term):
    first = base + term * NCH
    return [
        jnp.broadcast_to(ref[:, first + d : first + d + 1], (ROWS, LANES)) for d in range(NCH)
    ]


def mixed_item(weights, turns):
    return total([weights[d] * turns[d] for d in range(NCH)])


def mixed_items(weights, items):
    return [mixed_item(weights, turned(item)) for item in items]


FORWARD = 0
BACKWARD = TERMS * NCH


def near_forward(field, links, weights, partial, terms):
    for plane in range(PLANES):
        items = load_items(field, plane)
        sums = mixed_items(weight_rows(weights, FORWARD, 0), items)

        def add(term, hop, slot):
            mixed = mixed_items(weight_rows(weights, FORWARD, term), hop)
            for comp in range(COMPS):
                terms[slot, plane, comp] = hop[comp]
                sums[comp] = sums[comp] + mixed[comp]

        for direction in (2, 3):
            link = load_link(links, plane, direction)
            slot = 2 * (direction - 2)
            add(
                2 * direction + 1,
                hop_forward(link, step_items(items, direction, 1)),
                slot,
            )
            add(
                2 * direction + 2,
                step_items(hop_backward(link, items), direction, -1),
                slot + 1,
            )
        link = load_link(links, 0, 1)
        other = load_items(field, 1 - plane)
        if plane == 0:
            add(3, hop_forward(link, other), 4)
        else:
            add(4, hop_backward(link, other), 4)
        for comp in range(COMPS):
            partial[plane, comp] = sums[comp]


def store_items(ref, plane, items):
    for comp in range(COMPS):
        ref[plane, comp] = items[comp]


def store_message(ref, plane, items):
    for comp in range(COMPS):
        ref[plane * COMPS + comp] = items[comp]


def load_message(ref, plane):
    return [ref[plane * COMPS + comp] for comp in range(COMPS)]


def pack_forward(field_in, links_in, field, links, t_send, z_send, sems):
    copies = [
        pltpu.make_async_copy(links_in, links, sems.at[0]),
        pltpu.make_async_copy(field_in, field, sems.at[1]),
    ]
    for copy in copies:
        copy.start()
    for copy in copies:
        copy.wait()
    for plane in range(PLANES):
        items = load_items(field, plane)
        store_items(t_send, plane, hop_backward(load_link(links, plane, 0), items))
        if plane == 1:
            items = hop_backward(load_link(links, 1, 1), items)
        store_items(z_send, plane, items)


def far_forward(
    links, weights, loss, partial, t_next, t_prev, z_near, out, cot, terms, down, up, z_send
):
    for plane in range(PLANES):
        sums = load_items(partial, plane)

        def add(term, hop):
            mixed = mixed_items(weight_rows(weights, FORWARD, term), hop)
            for comp in range(COMPS):
                sums[comp] = sums[comp] + mixed[comp]

        if plane == 0:
            add(4, load_items(z_near, 1))
        else:
            hop = hop_forward(load_link(links, 1, 1), load_items(z_near, 0))
            store_items(terms, 2, hop)
            add(3, hop)
        t_link = load_link(links, plane, 0)
        hop = hop_forward(t_link, load_items(t_next, plane))
        store_items(terms, plane, hop)
        add(1, hop)
        add(2, load_items(t_prev, plane))
        row = loss[plane : plane + 1, :]
        scale = jnp.where(
            sublane_index() < NCH,
            jnp.broadcast_to(row[:, :LANES], (ROWS, LANES)),
            jnp.broadcast_to(row[:, LANES:], (ROWS, LANES)),
        )
        store_items(out, plane, sums)
        cots = [scale * item for item in sums]
        store_items(cot, plane, cots)
        turns = [turned(item) for item in cots]

        def pulled(direction, link):
            rows = weight_rows(weights, BACKWARD, 2 * direction + 1)
            return hop_backward(link, [mixed_item(rows, turn) for turn in turns])

        store_message(down, plane, cots)
        store_message(up, plane, pulled(0, t_link))
        store_items(z_send, plane, pulled(1, load_link(links, 1, 1)) if plane == 1 else cots)


def term_item(sources, term, plane, comp):
    field, near, far, t_prev, z_near = sources
    if term == 0:
        return field[plane, comp]
    if term == 1:
        return far[plane, comp]
    if term == 2:
        return t_prev[plane, comp]
    if term >= 5:
        return near[term - 5, plane, comp]
    if (term == 3) == (plane == 0):
        return near[4, plane, comp]
    return far[2, comp] if term == 3 else z_near[1, comp]


def weight_sums(sources, cot, sums, spread):
    sub = sublane_index()
    lane = lane_index()
    for channel in range(NCH):
        index = (sub & 4) + channel
        for plane in range(PLANES):
            for comp in range(COMPS):
                spread[channel, plane, comp] = pick_rows(cot[plane, comp], index)
    rows = [jnp.zeros((ROWS, LANES), F32) for _ in range(2)]
    for term in range(TERMS):
        parts = [None] * NCH
        for plane in range(PLANES):
            for comp in range(COMPS):
                value = term_item(sources, term, plane, comp)
                for channel in range(NCH):
                    piece = spread[channel, plane, comp] * value
                    parts[channel] = piece if parts[channel] is None else parts[channel] + piece
        for channel in range(NCH):
            summed = jnp.sum(parts[channel], axis=1, keepdims=True)
            place = lane == (channel >> 1) * LX + term
            rows[channel & 1] = jnp.where(place, summed, rows[channel & 1])
    even, odd = [row + pltpu.roll(row, NCH, axis=0) for row in rows]
    sums[...] = jnp.where(sub < NCH, even, odd)


def store_weight_grad(ref, tile):
    for channel in range(NCH):
        moved = pltpu.roll(tile, LANES - LX, axis=1) if channel >> 1 else tile
        first = (channel & 1) * NCH
        ref[channel] = moved[first : first + NCH, :TERMS]


def weight_partial(
    out_in, field, cot, near, far, t_prev, z_near, sums, out, spread, sem
):
    copy = pltpu.make_async_copy(out_in, out, sem)
    copy.start()
    weight_sums((field, near, far, t_prev, z_near), cot, sums, spread)
    copy.wait()


def near_backward(plane, links, weights, cot, partial):
    turns = [turned(cot[plane, comp]) for comp in range(COMPS)]

    def mixed(term):
        rows = weight_rows(weights, BACKWARD, term)
        return [mixed_item(rows, turn) for turn in turns]

    grads = mixed(0)

    def add(hop):
        for comp in range(COMPS):
            grads[comp] = grads[comp] + hop[comp]

    for direction in (2, 3):
        link = load_link(links, plane, direction)
        pulled = hop_backward(link, mixed(2 * direction + 1))
        add(step_items(pulled, direction, -1))
        add(hop_forward(link, step_items(mixed(2 * direction + 2), direction, 1)))
    link = load_link(links, 0, 1)
    term = 4 - plane
    other = mixed_items(weight_rows(weights, BACKWARD, term), load_items(cot, 1 - plane))
    add(hop_backward(link, other) if plane == 1 else hop_forward(link, other))
    for comp in range(COMPS):
        partial[comp] = grads[comp]


def far_backward(count, links, weights, first, second, t_next, t_prev, z_near, *refs):
    *sums, grad, weight_grad, held, held_sums, sems = refs
    tiles = [ref[...] for ref in sums]
    if len(tiles) == 2:
        tiles += [t_prev[PLANES * COMPS], t_next[PLANES * COMPS]]
    store_weight_grad(held_sums, paired_total(tiles) * (1.0 / count))
    copies = [pltpu.make_async_copy(held_sums, weight_grad, sems.at[PLANES])]
    copies[0].start()
    for plane, partial in enumerate((first, second)):
        grads = [partial[comp] for comp in range(COMPS)]

        def add(hop):
            for comp in range(COMPS):
                grads[comp] = grads[comp] + hop[comp]

        def pushed(direction, term, items):
            mixed = mixed_items(weight_rows(weights, BACKWARD, term), items)
            return hop_forward(load_link(links, plane, direction), mixed)

        add(pushed(1, 4, load_items(z_near, 0)) if plane == 1 else load_items(z_near, 1))
        add(load_message(t_prev, plane))
        add(pushed(0, 2, load_message(t_next, plane)))
        store_items(held, plane, grads)
        copies.append(pltpu.make_async_copy(held.at[plane], grad.at[plane], sems.at[plane]))
        copies[-1].start()
    for copy in copies:
        copy.wait()


def attach_sums(down_in, up_in, *refs):
    *near_sums, down, up, sums = refs
    tile = paired_total([ref[...] for ref in near_sums])
    for ref in (down, up):
        ref[PLANES * COMPS] = tile
    sums[...] = tile


def run(kernel, shapes, *operands, scratch=(), in_hbm=(), out_hbm=(), aliases=()):
    def place(in_far):
        space = pltpu.HBM if in_far else pltpu.VMEM
        return pl.BlockSpec(memory_space=space)

    return pl.pallas_call(
        kernel,
        out_shape=[jax.ShapeDtypeStruct(shape, F32) for shape in shapes],
        in_specs=[place(i in in_hbm) for i in range(len(operands))],
        out_specs=[place(i in out_hbm) for i in range(len(shapes))],
        scratch_shapes=list(scratch),
        input_output_aliases=dict(aliases),
        compiler_params=pltpu.CompilerParams(vmem_limit_bytes=32 * 2**20),
    )(*operands)


def shifted(value, axis, offset):
    count = lax.axis_size(axis)
    return lax.ppermute(value, axis, [(i, (i + offset) % count) for i in range(count)])


def z_planes(block):
    if lax.axis_size("gz") == 2:
        return shifted(block, "gz", 1)
    return jnp.concatenate([shifted(block[:1], "gz", -1), shifted(block[1:], "gz", 1)], axis=0)


def partners(value, axes):
    count = 1
    for axis in axes:
        count *= lax.axis_size(axis)
    if count == 4:
        moved = [lax.ppermute(value, axes, [(i, i ^ k) for i in range(4)]) for k in (1, 2, 3)]
        return [value] + moved
    for axis in axes:
        size = lax.axis_size(axis)
        if size & (size - 1):
            value = lax.psum(value, axis)
            continue
        step = 1
        while step < size:
            value = value + lax.ppermute(value, axis, [(i, i ^ step) for i in range(size)])
            step *= 2
    return [value]


def paired_total(values):
    while len(values) > 1:
        values = [a + b for a, b in zip(values[::2], values[1::2])]
    return values[0]


def weight_table(conv_weights):
    out_index, in_index, turn = np.indices((NCH, NCH, NCH))
    forward_pick = ((out_index + turn) % NCH == in_index).astype(np.float32)
    backward_pick = ((in_index + turn) % NCH == out_index).astype(np.float32)
    wide = conv_weights[:, :, :, None]
    forward = jnp.sum(wide * forward_pick[:, :, None, :], axis=1)
    backward = jnp.sum(wide * backward_pick[:, :, None, :], axis=0)
    table = jnp.concatenate(
        [forward.reshape(NCH, TERMS * NCH), backward.reshape(NCH, TERMS * NCH)], axis=1
    )
    return jnp.concatenate([table, table], axis=0)


def local(gauge_links, input_field, conv_weights, loss_weight):
    shape = input_field.shape
    field_in = to_rows(input_field)
    t_next = shifted(field_in, "ta", -1)
    field, links, t_send, z_send = run(
        pack_forward,
        (FIELD,) * 4,
        pltpu.with_memory_space_constraint(field_in, pltpu.HBM),
        pltpu.with_memory_space_constraint(to_rows(gauge_links), pltpu.HBM),
        scratch=[pltpu.SemaphoreType.DMA((2,))],
        in_hbm=(0, 1),
    )
    t_prev = shifted(t_send, "ta", 1)
    z_near = z_planes(z_send)
    weights = weight_table(conv_weights)
    loss = loss_weight.reshape(PLANES, HALF * LANES)
    partial, near = run(near_forward, (FIELD, (5,) + FIELD), field, links, weights)
    out, cot, far, down, up, z_send = run(
        far_forward,
        (FIELD, FIELD, (3,) + FIELD[1:], MESSAGE, MESSAGE, FIELD),
        links,
        weights,
        loss,
        partial,
        t_next,
        t_prev,
        z_near,
    )
    sums, out = run(
        weight_partial,
        (TILE, FIELD),
        out,
        field,
        cot,
        near,
        far,
        t_prev,
        z_near,
        scratch=[pltpu.VMEM((NCH,) + FIELD, F32), pltpu.SemaphoreType.DMA],
        out_hbm=(1,),
    )
    down, up, sums = run(
        attach_sums,
        (MESSAGE, MESSAGE, TILE),
        down,
        up,
        *partners(sums, ("gz", "rep")),
        aliases=((0, 0), (1, 1)),
    )
    t_next_cot = shifted(down, "ta", -1)
    t_prev_cot = shifted(up, "ta", 1)
    z_near_cot = z_planes(z_send)
    if lax.axis_size("ta") == 4:
        all_sums = [sums, shifted(sums, "ta", 2)]
    else:
        all_sums = [paired_total(partners(sums, ("ta",)))]
    halves = [
        run(functools.partial(near_backward, plane), (FIELD[1:],), links, weights, cot)[0]
        for plane in range(PLANES)
    ]
    count = loss_weight.size
    for axis in ("ta", "gz", "rep"):
        count = count * lax.axis_size(axis)
    grad, weight_grad = run(
        functools.partial(far_backward, count),
        (FIELD, (NCH, NCH, TERMS)),
        links,
        weights,
        *halves,
        t_next_cot,
        t_prev_cot,
        z_near_cot,
        *all_sums,
        scratch=[
            pltpu.VMEM(FIELD, F32),
            pltpu.VMEM((NCH, NCH, TERMS), F32),
            pltpu.SemaphoreType.DMA((PLANES + 1,)),
        ],
        out_hbm=(0, 1),
    )
    return from_rows(out, shape), from_rows(grad, shape), weight_grad


def solution(mesh):
    split = P(("groups", "rep"), "ta", "gz", None, None, None, None, None)
    return jax.shard_map(
        local,
        mesh=mesh,
        in_specs=(split, split, P(), P(("groups", "rep"), "ta", "gz", None)),
        out_specs=(split, split, P("groups", None, None)),
        check_vma=False,
    )
```

```python
import functools

import jax
import jax.numpy as jnp
import numpy as np
from jax import lax
from jax.experimental import pallas as pl
from jax.experimental.pallas import tpu as pltpu
from jax.sharding import PartitionSpec as P

PLANES = 2
NCH = 4
TERMS = 9
COMPS = 18
HALF = 2
ROWS = HALF * NCH
LANES = 128
LX = 16
FIELD = (PLANES, COMPS, ROWS, LANES)
MESSAGE = (PLANES * COMPS + 1, ROWS, LANES)
TILE = (ROWS, LANES)
F32 = jnp.float32


def to_rows(block):
    planes = block.size // (COMPS * ROWS * LANES)
    split = block.reshape(planes, COMPS, NCH, HALF, LANES)
    return split.transpose(0, 1, 3, 2, 4).reshape(planes, COMPS, ROWS, LANES)


def from_rows(rows, shape):
    split = rows.reshape(PLANES, COMPS, HALF, NCH, LANES)
    return split.transpose(0, 1, 3, 2, 4).reshape(shape)


def sublane_index():
    return lax.broadcasted_iota(jnp.int32, (ROWS, LANES), 0)


def lane_index():
    return lax.broadcasted_iota(jnp.int32, (ROWS, LANES), 1)


def pick_rows(value, index):
    return jnp.take_along_axis(value, index, axis=0, mode="promise_in_bounds")


def as_matrix(items):
    return [[[items[p * 9 + r * 3 + c] for c in range(3)] for r in range(3)] for p in range(2)]


def as_items(matrix):
    return [matrix[p][r][c] for p in range(2) for r in range(3) for c in range(3)]


def total(items):
    result = items[0]
    for item in items[1:]:
        result = result + item
    return result


def product(left, right):
    (lr, li), (rr, ri) = left, right
    out = [[], []]
    for r in range(3):
        out[0].append(
            [
                total([lr[r][k] * rr[k][c] for k in range(3)])
                - total([li[r][k] * ri[k][c] for k in range(3)])
                for c in range(3)
            ]
        )
        out[1].append(
            [
                total([lr[r][k] * ri[k][c] for k in range(3)])
                + total([li[r][k] * rr[k][c] for k in range(3)])
                for c in range(3)
            ]
        )
    return out


def product_left_dagger(left, right):
    (lr, li), (rr, ri) = left, right
    out = [[], []]
    for r in range(3):
        out[0].append(
            [
                total([lr[k][r] * rr[k][c] for k in range(3)])
                + total([li[k][r] * ri[k][c] for k in range(3)])
                for c in range(3)
            ]
        )
        out[1].append(
            [
                total([lr[k][r] * ri[k][c] for k in range(3)])
                - total([li[k][r] * rr[k][c] for k in range(3)])
                for c in range(3)
            ]
        )
    return out


def product_right_dagger(left, right):
    (lr, li), (rr, ri) = left, right
    out = [[], []]
    for r in range(3):
        out[0].append(
            [
                total([lr[r][k] * rr[c][k] for k in range(3)])
                + total([li[r][k] * ri[c][k] for k in range(3)])
                for c in range(3)
            ]
        )
        out[1].append(
            [
                total([li[r][k] * rr[c][k] for k in range(3)])
                - total([lr[r][k] * ri[c][k] for k in range(3)])
                for c in range(3)
            ]
        )
    return out


def hop_forward(link, items):
    matrix = as_matrix(items)
    return as_items(product_right_dagger(product(link, matrix), link))


def hop_backward(link, items):
    matrix = as_matrix(items)
    return as_items(product(product_left_dagger(link, matrix), link))


def load_items(ref, plane):
    return [ref[plane, comp] for comp in range(COMPS)]


def load_link(ref, plane, direction):
    index = (sublane_index() & 4) + direction
    return as_matrix([pick_rows(ref[plane, comp], index) for comp in range(COMPS)])


def step_plane(value, direction, offset):
    lane = lane_index()
    if direction == 3:
        inner = lane & (LX - 1)
        if offset > 0:
            return jnp.where(
                inner == LX - 1,
                pltpu.roll(value, LX - 1, axis=1),
                pltpu.roll(value, LANES - 1, axis=1),
            )
        return jnp.where(
            inner == 0,
            pltpu.roll(value, LANES - LX + 1, axis=1),
            pltpu.roll(value, 1, axis=1),
        )
    if offset > 0:
        moved = pltpu.roll(value, LANES - LX, axis=1)
        return jnp.where(lane >= LANES - LX, pltpu.roll(moved, NCH, axis=0), moved)
    moved = pltpu.roll(value, LX, axis=1)
    return jnp.where(lane < LX, pltpu.roll(moved, NCH, axis=0), moved)


def step_items(items, direction, offset):
    return [step_plane(item, direction, offset) for item in items]


def turned(value):
    sub = sublane_index()
    return [value] + [pick_rows(value, (sub & 4) | ((sub + d) & 3)) for d in range(1, NCH)]


def weight_rows(ref, base, term):
    first = base + term * NCH
    return [
        jnp.broadcast_to(ref[:, first + d : first + d + 1], (ROWS, LANES)) for d in range(NCH)
    ]


def mixed_item(weights, turns):
    return total([weights[d] * turns[d] for d in range(NCH)])


def mixed_items(weights, items):
    return [mixed_item(weights, turned(item)) for item in items]


FORWARD = 0
BACKWARD = TERMS * NCH


def near_forward(field, links, weights, partial, terms):
    for plane in range(PLANES):
        items = load_items(field, plane)
        sums = mixed_items(weight_rows(weights, FORWARD, 0), items)

        def add(term, hop, slot):
            mixed = mixed_items(weight_rows(weights, FORWARD, term), hop)
            for comp in range(COMPS):
                terms[slot, plane, comp] = hop[comp]
                sums[comp] = sums[comp] + mixed[comp]

        for direction in (2, 3):
            link = load_link(links, plane, direction)
            slot = 2 * (direction - 2)
            add(
                2 * direction + 1,
                hop_forward(link, step_items(items, direction, 1)),
                slot,
            )
            add(
                2 * direction + 2,
                step_items(hop_backward(link, items), direction, -1),
                slot + 1,
            )
        link = load_link(links, 0, 1)
        other = load_items(field, 1 - plane)
        if plane == 0:
            add(3, hop_forward(link, other), 4)
        else:
            add(4, hop_backward(link, other), 4)
        for comp in range(COMPS):
            partial[plane, comp] = sums[comp]


def store_items(ref, plane, items):
    for comp in range(COMPS):
        ref[plane, comp] = items[comp]


def store_message(ref, plane, items):
    for comp in range(COMPS):
        ref[plane * COMPS + comp] = items[comp]


def load_message(ref, plane):
    return [ref[plane * COMPS + comp] for comp in range(COMPS)]


def pack_forward(field_in, links_in, field, links, t_send, z_send, sems):
    copies = [
        pltpu.make_async_copy(links_in, links, sems.at[0]),
        pltpu.make_async_copy(field_in, field, sems.at[1]),
    ]
    for copy in copies:
        copy.start()
    for copy in copies:
        copy.wait()
    for plane in range(PLANES):
        items = load_items(field, plane)
        store_items(t_send, plane, hop_backward(load_link(links, plane, 0), items))
        if plane == 1:
            items = hop_backward(load_link(links, 1, 1), items)
        store_items(z_send, plane, items)


def far_forward(
    links, weights, loss, partial, t_next, t_prev, z_near, out, cot, terms, down, up, z_send
):
    for plane in range(PLANES):
        sums = load_items(partial, plane)

        def add(term, hop):
            mixed = mixed_items(weight_rows(weights, FORWARD, term), hop)
            for comp in range(COMPS):
                sums[comp] = sums[comp] + mixed[comp]

        if plane == 0:
            add(4, load_items(z_near, 1))
        else:
            hop = hop_forward(load_link(links, 1, 1), load_items(z_near, 0))
            store_items(terms, 2, hop)
            add(3, hop)
        t_link = load_link(links, plane, 0)
        hop = hop_forward(t_link, load_items(t_next, plane))
        store_items(terms, plane, hop)
        add(1, hop)
        add(2, load_items(t_prev, plane))
        row = loss[plane : plane + 1, :]
        scale = jnp.where(
            sublane_index() < NCH,
            jnp.broadcast_to(row[:, :LANES], (ROWS, LANES)),
            jnp.broadcast_to(row[:, LANES:], (ROWS, LANES)),
        )
        store_items(out, plane, sums)
        cots = [scale * item for item in sums]
        store_items(cot, plane, cots)
        turns = [turned(item) for item in cots]

        def pulled(direction, link):
            rows = weight_rows(weights, BACKWARD, 2 * direction + 1)
            return hop_backward(link, [mixed_item(rows, turn) for turn in turns])

        store_message(down, plane, cots)
        store_message(up, plane, pulled(0, t_link))
        store_items(z_send, plane, pulled(1, load_link(links, 1, 1)) if plane == 1 else cots)


def term_item(sources, term, plane, comp):
    field, near, far, t_prev, z_near = sources
    if term == 0:
        return field[plane, comp]
    if term == 1:
        return far[plane, comp]
    if term == 2:
        return t_prev[plane, comp]
    if term >= 5:
        return near[term - 5, plane, comp]
    if (term == 3) == (plane == 0):
        return near[4, plane, comp]
    return far[2, comp] if term == 3 else z_near[1, comp]


def weight_sums(sources, cot, sums, spread):
    sub = sublane_index()
    lane = lane_index()
    for channel in range(NCH):
        index = (sub & 4) + channel
        for plane in range(PLANES):
            for comp in range(COMPS):
                spread[channel, plane, comp] = pick_rows(cot[plane, comp], index)
    rows = [jnp.zeros((ROWS, LANES), F32) for _ in range(2)]
    for term in range(TERMS):
        parts = [None] * NCH
        for plane in range(PLANES):
            for comp in range(COMPS):
                value = term_item(sources, term, plane, comp)
                for channel in range(NCH):
                    piece = spread[channel, plane, comp] * value
                    parts[channel] = piece if parts[channel] is None else parts[channel] + piece
        for channel in range(NCH):
            summed = jnp.sum(parts[channel], axis=1, keepdims=True)
            place = lane == (channel >> 1) * LX + term
            rows[channel & 1] = jnp.where(place, summed, rows[channel & 1])
    even, odd = [row + pltpu.roll(row, NCH, axis=0) for row in rows]
    sums[...] = jnp.where(sub < NCH, even, odd)


def store_weight_grad(ref, tile):
    for channel in range(NCH):
        moved = pltpu.roll(tile, LANES - LX, axis=1) if channel >> 1 else tile
        first = (channel & 1) * NCH
        ref[channel] = moved[first : first + NCH, :TERMS]


def weight_partial(
    out_in, field, cot, near, far, t_prev, z_near, *refs
):
    down, up, sums, out, spread, sem = refs[2:]
    copy = pltpu.make_async_copy(out_in, out, sem)
    copy.start()
    weight_sums((field, near, far, t_prev, z_near), cot, sums, spread)
    for ref in (down, up):
        ref[PLANES * COMPS] = sums[...]
    copy.wait()


def near_backward(plane, links, weights, cot, partial):
    turns = [turned(cot[plane, comp]) for comp in range(COMPS)]

    def mixed(term):
        rows = weight_rows(weights, BACKWARD, term)
        return [mixed_item(rows, turn) for turn in turns]

    grads = mixed(0)

    def add(hop):
        for comp in range(COMPS):
            grads[comp] = grads[comp] + hop[comp]

    for direction in (2, 3):
        link = load_link(links, plane, direction)
        pulled = hop_backward(link, mixed(2 * direction + 1))
        add(step_items(pulled, direction, -1))
        add(hop_forward(link, step_items(mixed(2 * direction + 2), direction, 1)))
    link = load_link(links, 0, 1)
    term = 4 - plane
    other = mixed_items(weight_rows(weights, BACKWARD, term), load_items(cot, 1 - plane))
    add(hop_backward(link, other) if plane == 1 else hop_forward(link, other))
    for comp in range(COMPS):
        partial[comp] = grads[comp]


def far_backward(links, weights, first, second, t_next, t_prev, z_near, grad, held, sems):
    copies = []
    for plane, partial in enumerate((first, second)):
        grads = [partial[comp] for comp in range(COMPS)]

        def add(hop):
            for comp in range(COMPS):
                grads[comp] = grads[comp] + hop[comp]

        def pushed(direction, term, items):
            mixed = mixed_items(weight_rows(weights, BACKWARD, term), items)
            return hop_forward(load_link(links, plane, direction), mixed)

        add(pushed(1, 4, load_items(z_near, 0)) if plane == 1 else load_items(z_near, 1))
        add(load_message(t_prev, plane))
        add(pushed(0, 2, load_message(t_next, plane)))
        store_items(held, plane, grads)
        copies.append(pltpu.make_async_copy(held.at[plane], grad.at[plane], sems.at[plane]))
        copies[-1].start()
    for copy in copies:
        copy.wait()


def line_sums(own, opposite, t_next, t_prev, sums):
    last = PLANES * COMPS
    sums[...] = (own[...] + opposite[...]) + (t_prev[last] + t_next[last])


def all_sums(count, *refs):
    tile = paired_total([ref[...] for ref in refs[:-1]])
    store_weight_grad(refs[-1], tile * (1.0 / count))


def run(kernel, shapes, *operands, scratch=(), in_hbm=(), out_hbm=(), aliases=()):
    def place(in_far):
        space = pltpu.HBM if in_far else pltpu.VMEM
        return pl.BlockSpec(memory_space=space)

    return pl.pallas_call(
        kernel,
        out_shape=[jax.ShapeDtypeStruct(shape, F32) for shape in shapes],
        in_specs=[place(i in in_hbm) for i in range(len(operands))],
        out_specs=[place(i in out_hbm) for i in range(len(shapes))],
        scratch_shapes=list(scratch),
        input_output_aliases=dict(aliases),
        compiler_params=pltpu.CompilerParams(vmem_limit_bytes=32 * 2**20),
    )(*operands)


def shifted(value, axis, offset):
    count = lax.axis_size(axis)
    return lax.ppermute(value, axis, [(i, (i + offset) % count) for i in range(count)])


def z_planes(block):
    if lax.axis_size("gz") == 2:
        return shifted(block, "gz", 1)
    return jnp.concatenate([shifted(block[:1], "gz", -1), shifted(block[1:], "gz", 1)], axis=0)


def partners(value, axes):
    count = 1
    for axis in axes:
        count *= lax.axis_size(axis)
    if count == 4:
        moved = [lax.ppermute(value, axes, [(i, i ^ k) for i in range(4)]) for k in (1, 2, 3)]
        return [value] + moved
    for axis in axes:
        size = lax.axis_size(axis)
        if size & (size - 1):
            value = lax.psum(value, axis)
            continue
        step = 1
        while step < size:
            value = value + lax.ppermute(value, axis, [(i, i ^ step) for i in range(size)])
            step *= 2
    return [value]


def paired_total(values):
    while len(values) > 1:
        values = [a + b for a, b in zip(values[::2], values[1::2])]
    return values[0]


def weight_table(conv_weights):
    out_index, in_index, turn = np.indices((NCH, NCH, NCH))
    forward_pick = ((out_index + turn) % NCH == in_index).astype(np.float32)
    backward_pick = ((in_index + turn) % NCH == out_index).astype(np.float32)
    wide = conv_weights[:, :, :, None]
    forward = jnp.sum(wide * forward_pick[:, :, None, :], axis=1)
    backward = jnp.sum(wide * backward_pick[:, :, None, :], axis=0)
    table = jnp.concatenate(
        [forward.reshape(NCH, TERMS * NCH), backward.reshape(NCH, TERMS * NCH)], axis=1
    )
    return jnp.concatenate([table, table], axis=0)


def local(gauge_links, input_field, conv_weights, loss_weight):
    shape = input_field.shape
    field_in = to_rows(input_field)
    t_next = shifted(field_in, "ta", -1)
    field, links, t_send, z_send = run(
        pack_forward,
        (FIELD,) * 4,
        pltpu.with_memory_space_constraint(field_in, pltpu.HBM),
        pltpu.with_memory_space_constraint(to_rows(gauge_links), pltpu.HBM),
        scratch=[pltpu.SemaphoreType.DMA((2,))],
        in_hbm=(0, 1),
    )
    t_prev = shifted(t_send, "ta", 1)
    z_near = z_planes(z_send)
    weights = weight_table(conv_weights)
    loss = loss_weight.reshape(PLANES, HALF * LANES)
    partial, near = run(near_forward, (FIELD, (5,) + FIELD), field, links, weights)
    out, cot, far, down, up, z_send = run(
        far_forward,
        (FIELD, FIELD, (3,) + FIELD[1:], MESSAGE, MESSAGE, FIELD),
        links,
        weights,
        loss,
        partial,
        t_next,
        t_prev,
        z_near,
    )
    down, up, sums, out = run(
        weight_partial,
        (MESSAGE, MESSAGE, TILE, FIELD),
        out,
        field,
        cot,
        near,
        far,
        t_prev,
        z_near,
        down,
        up,
        scratch=[pltpu.VMEM((NCH,) + FIELD, F32), pltpu.SemaphoreType.DMA],
        out_hbm=(3,),
        aliases=((7, 0), (8, 1)),
    )
    t_next_cot = shifted(down, "ta", -1)
    t_prev_cot = shifted(up, "ta", 1)
    z_near_cot = z_planes(z_send)
    if lax.axis_size("ta") == 4:
        opposite = shifted(sums, "ta", 2)
    else:
        sums = paired_total(partners(sums, ("ta",)))
    halves = [
        run(functools.partial(near_backward, plane), (FIELD[1:],), links, weights, cot)[0]
        for plane in range(PLANES)
    ]
    sums, *halves = lax.optimization_barrier((sums, *halves))
    if lax.axis_size("ta") == 4:
        (sums,) = run(line_sums, (TILE,), sums, opposite, t_next_cot, t_prev_cot)
    count = loss_weight.size
    for axis in ("ta", "gz", "rep"):
        count = count * lax.axis_size(axis)
    (weight_grad,) = run(
        functools.partial(all_sums, count),
        ((NCH, NCH, TERMS),),
        *partners(sums, ("gz", "rep")),
    )
    (grad,) = run(
        far_backward,
        (FIELD,),
        links,
        weights,
        *halves,
        t_next_cot,
        t_prev_cot,
        z_near_cot,
        scratch=[pltpu.VMEM(FIELD, F32), pltpu.SemaphoreType.DMA((PLANES,))],
        out_hbm=(0,),
    )
    return from_rows(out, shape), from_rows(grad, shape), weight_grad


def solution(mesh):
    split = P(("groups", "rep"), "ta", "gz", None, None, None, None, None)
    return jax.shard_map(
        local,
        mesh=mesh,
        in_specs=(split, split, P(), P(("groups", "rep"), "ta", "gz", None)),
        out_specs=(split, split, P("groups", None, None)),
        check_vma=False,
    )
```

```python
import functools

import jax
import jax.numpy as jnp
import numpy as np
from jax import lax
from jax.experimental import pallas as pl
from jax.experimental.pallas import tpu as pltpu
from jax.sharding import PartitionSpec as P

PLANES = 2
NCH = 4
TERMS = 9
COMPS = 18
HALF = 2
ROWS = HALF * NCH
LANES = 128
LX = 16
FIELD = (PLANES, COMPS, ROWS, LANES)
MESSAGE = (PLANES * COMPS + 1, ROWS, LANES)
TILE = (ROWS, LANES)
F32 = jnp.float32


def to_rows(block):
    planes = block.size // (COMPS * ROWS * LANES)
    split = block.reshape(planes, COMPS, NCH, HALF, LANES)
    return split.transpose(0, 1, 3, 2, 4).reshape(planes, COMPS, ROWS, LANES)


def from_rows(rows, shape):
    split = rows.reshape(PLANES, COMPS, HALF, NCH, LANES)
    return split.transpose(0, 1, 3, 2, 4).reshape(shape)


def sublane_index():
    return lax.broadcasted_iota(jnp.int32, (ROWS, LANES), 0)


def lane_index():
    return lax.broadcasted_iota(jnp.int32, (ROWS, LANES), 1)


def pick_rows(value, index):
    return jnp.take_along_axis(value, index, axis=0, mode="promise_in_bounds")


def as_matrix(items):
    return [[[items[p * 9 + r * 3 + c] for c in range(3)] for r in range(3)] for p in range(2)]


def as_items(matrix):
    return [matrix[p][r][c] for p in range(2) for r in range(3) for c in range(3)]


def total(items):
    result = items[0]
    for item in items[1:]:
        result = result + item
    return result


def product(left, right):
    (lr, li), (rr, ri) = left, right
    out = [[], []]
    for r in range(3):
        out[0].append(
            [
                total([lr[r][k] * rr[k][c] for k in range(3)])
                - total([li[r][k] * ri[k][c] for k in range(3)])
                for c in range(3)
            ]
        )
        out[1].append(
            [
                total([lr[r][k] * ri[k][c] for k in range(3)])
                + total([li[r][k] * rr[k][c] for k in range(3)])
                for c in range(3)
            ]
        )
    return out


def product_left_dagger(left, right):
    (lr, li), (rr, ri) = left, right
    out = [[], []]
    for r in range(3):
        out[0].append(
            [
                total([lr[k][r] * rr[k][c] for k in range(3)])
                + total([li[k][r] * ri[k][c] for k in range(3)])
                for c in range(3)
            ]
        )
        out[1].append(
            [
                total([lr[k][r] * ri[k][c] for k in range(3)])
                - total([li[k][r] * rr[k][c] for k in range(3)])
                for c in range(3)
            ]
        )
    return out


def product_right_dagger(left, right):
    (lr, li), (rr, ri) = left, right
    out = [[], []]
    for r in range(3):
        out[0].append(
            [
                total([lr[r][k] * rr[c][k] for k in range(3)])
                + total([li[r][k] * ri[c][k] for k in range(3)])
                for c in range(3)
            ]
        )
        out[1].append(
            [
                total([li[r][k] * rr[c][k] for k in range(3)])
                - total([lr[r][k] * ri[c][k] for k in range(3)])
                for c in range(3)
            ]
        )
    return out


def hop_forward(link, items):
    matrix = as_matrix(items)
    return as_items(product_right_dagger(product(link, matrix), link))


def hop_backward(link, items):
    matrix = as_matrix(items)
    return as_items(product(product_left_dagger(link, matrix), link))


def load_items(ref, plane):
    return [ref[plane, comp] for comp in range(COMPS)]


def load_link(ref, plane, direction):
    index = (sublane_index() & 4) + direction
    return as_matrix([pick_rows(ref[plane, comp], index) for comp in range(COMPS)])


def step_plane(value, direction, offset):
    lane = lane_index()
    if direction == 3:
        inner = lane & (LX - 1)
        if offset > 0:
            return jnp.where(
                inner == LX - 1,
                pltpu.roll(value, LX - 1, axis=1),
                pltpu.roll(value, LANES - 1, axis=1),
            )
        return jnp.where(
            inner == 0,
            pltpu.roll(value, LANES - LX + 1, axis=1),
            pltpu.roll(value, 1, axis=1),
        )
    if offset > 0:
        moved = pltpu.roll(value, LANES - LX, axis=1)
        return jnp.where(lane >= LANES - LX, pltpu.roll(moved, NCH, axis=0), moved)
    moved = pltpu.roll(value, LX, axis=1)
    return jnp.where(lane < LX, pltpu.roll(moved, NCH, axis=0), moved)


def step_items(items, direction, offset):
    return [step_plane(item, direction, offset) for item in items]


def turned(value):
    sub = sublane_index()
    return [value] + [pick_rows(value, (sub & 4) | ((sub + d) & 3)) for d in range(1, NCH)]


def weight_rows(ref, base, term):
    first = base + term * NCH
    return [
        jnp.broadcast_to(ref[:, first + d : first + d + 1], (ROWS, LANES)) for d in range(NCH)
    ]


def mixed_item(weights, turns):
    return total([weights[d] * turns[d] for d in range(NCH)])


def mixed_items(weights, items):
    return [mixed_item(weights, turned(item)) for item in items]


FORWARD = 0
BACKWARD = TERMS * NCH


def near_forward(field, links, weights, partial, terms):
    for plane in range(PLANES):
        items = load_items(field, plane)
        sums = mixed_items(weight_rows(weights, FORWARD, 0), items)

        def add(term, hop, slot):
            mixed = mixed_items(weight_rows(weights, FORWARD, term), hop)
            for comp in range(COMPS):
                terms[slot, plane, comp] = hop[comp]
                sums[comp] = sums[comp] + mixed[comp]

        for direction in (2, 3):
            link = load_link(links, plane, direction)
            slot = 2 * (direction - 2)
            add(
                2 * direction + 1,
                hop_forward(link, step_items(items, direction, 1)),
                slot,
            )
            add(
                2 * direction + 2,
                step_items(hop_backward(link, items), direction, -1),
                slot + 1,
            )
        link = load_link(links, 0, 1)
        other = load_items(field, 1 - plane)
        if plane == 0:
            add(3, hop_forward(link, other), 4)
        else:
            add(4, hop_backward(link, other), 4)
        for comp in range(COMPS):
            partial[plane, comp] = sums[comp]


def store_items(ref, plane, items):
    for comp in range(COMPS):
        ref[plane, comp] = items[comp]


def store_message(ref, plane, items):
    for comp in range(COMPS):
        ref[plane * COMPS + comp] = items[comp]


def load_message(ref, plane):
    return [ref[plane * COMPS + comp] for comp in range(COMPS)]


def pack_forward(field_in, links_in, field, links, t_send, z_send, sems):
    copies = [
        pltpu.make_async_copy(links_in, links, sems.at[0]),
        pltpu.make_async_copy(field_in, field, sems.at[1]),
    ]
    for copy in copies:
        copy.start()
    for copy in copies:
        copy.wait()
    for plane in range(PLANES):
        items = load_items(field, plane)
        store_items(t_send, plane, hop_backward(load_link(links, plane, 0), items))
        if plane == 1:
            items = hop_backward(load_link(links, 1, 1), items)
        store_items(z_send, plane, items)


def far_forward(
    links, weights, loss, partial, t_next, t_prev, z_near, out, cot, terms, down, up, z_send
):
    for plane in range(PLANES):
        sums = load_items(partial, plane)

        def add(term, hop):
            mixed = mixed_items(weight_rows(weights, FORWARD, term), hop)
            for comp in range(COMPS):
                sums[comp] = sums[comp] + mixed[comp]

        if plane == 0:
            add(4, load_items(z_near, 1))
        else:
            hop = hop_forward(load_link(links, 1, 1), load_items(z_near, 0))
            store_items(terms, 2, hop)
            add(3, hop)
        t_link = load_link(links, plane, 0)
        hop = hop_forward(t_link, load_items(t_next, plane))
        store_items(terms, plane, hop)
        add(1, hop)
        add(2, load_items(t_prev, plane))
        row = loss[plane : plane + 1, :]
        scale = jnp.where(
            sublane_index() < NCH,
            jnp.broadcast_to(row[:, :LANES], (ROWS, LANES)),
            jnp.broadcast_to(row[:, LANES:], (ROWS, LANES)),
        )
        store_items(out, plane, sums)
        cots = [scale * item for item in sums]
        store_items(cot, plane, cots)
        turns = [turned(item) for item in cots]

        def pulled(direction, link):
            rows = weight_rows(weights, BACKWARD, 2 * direction + 1)
            return hop_backward(link, [mixed_item(rows, turn) for turn in turns])

        store_message(down, plane, cots)
        store_message(up, plane, pulled(0, t_link))
        store_items(z_send, plane, pulled(1, load_link(links, 1, 1)) if plane == 1 else cots)


def term_item(sources, term, plane, comp):
    field, near, far, t_prev, z_near = sources
    if term == 0:
        return field[plane, comp]
    if term == 1:
        return far[plane, comp]
    if term == 2:
        return t_prev[plane, comp]
    if term >= 5:
        return near[term - 5, plane, comp]
    if (term == 3) == (plane == 0):
        return near[4, plane, comp]
    return far[2, comp] if term == 3 else z_near[1, comp]


def weight_sums(sources, cot, sums, spread):
    sub = sublane_index()
    lane = lane_index()
    for channel in range(NCH):
        index = (sub & 4) + channel
        for plane in range(PLANES):
            for comp in range(COMPS):
                spread[channel, plane, comp] = pick_rows(cot[plane, comp], index)
    rows = [jnp.zeros((ROWS, LANES), F32) for _ in range(2)]
    for term in range(TERMS):
        parts = [None] * NCH
        for plane in range(PLANES):
            for comp in range(COMPS):
                value = term_item(sources, term, plane, comp)
                for channel in range(NCH):
                    piece = spread[channel, plane, comp] * value
                    parts[channel] = piece if parts[channel] is None else parts[channel] + piece
        for channel in range(NCH):
            summed = jnp.sum(parts[channel], axis=1, keepdims=True)
            place = lane == (channel >> 1) * LX + term
            rows[channel & 1] = jnp.where(place, summed, rows[channel & 1])
    even, odd = [row + pltpu.roll(row, NCH, axis=0) for row in rows]
    sums[...] = jnp.where(sub < NCH, even, odd)


def store_weight_grad(ref, tile):
    for channel in range(NCH):
        moved = pltpu.roll(tile, LANES - LX, axis=1) if channel >> 1 else tile
        first = (channel & 1) * NCH
        ref[channel] = moved[first : first + NCH, :TERMS]


def weight_partial(field, cot, near, far, t_prev, z_near, *refs):
    down, up, sums, spread = refs[2:]
    weight_sums((field, near, far, t_prev, z_near), cot, sums, spread)
    for ref in (down, up):
        ref[PLANES * COMPS] = sums[...]


def near_backward(out_in, links, weights, cot, out, partial, sem):
    copy = pltpu.make_async_copy(out_in, out, sem)
    copy.start()
    for plane in range(PLANES):
        near_backward_plane(plane, links, weights, cot, partial)
    copy.wait()


def near_backward_plane(plane, links, weights, cot, partial):
    turns = [turned(cot[plane, comp]) for comp in range(COMPS)]

    def mixed(term):
        rows = weight_rows(weights, BACKWARD, term)
        return [mixed_item(rows, turn) for turn in turns]

    grads = mixed(0)

    def add(hop):
        for comp in range(COMPS):
            grads[comp] = grads[comp] + hop[comp]

    for direction in (2, 3):
        link = load_link(links, plane, direction)
        pulled = hop_backward(link, mixed(2 * direction + 1))
        add(step_items(pulled, direction, -1))
        add(hop_forward(link, step_items(mixed(2 * direction + 2), direction, 1)))
    link = load_link(links, 0, 1)
    term = 4 - plane
    other = mixed_items(weight_rows(weights, BACKWARD, term), load_items(cot, 1 - plane))
    add(hop_backward(link, other) if plane == 1 else hop_forward(link, other))
    for comp in range(COMPS):
        partial[plane, comp] = grads[comp]


def far_backward(links, weights, partial, t_next, t_prev, z_near, grad, held, sems):
    copies = []
    for plane in range(PLANES):
        grads = load_items(partial, plane)

        def add(hop):
            for comp in range(COMPS):
                grads[comp] = grads[comp] + hop[comp]

        def pushed(direction, term, items):
            mixed = mixed_items(weight_rows(weights, BACKWARD, term), items)
            return hop_forward(load_link(links, plane, direction), mixed)

        add(pushed(1, 4, load_items(z_near, 0)) if plane == 1 else load_items(z_near, 1))
        add(load_message(t_prev, plane))
        add(pushed(0, 2, load_message(t_next, plane)))
        store_items(held, plane, grads)
        copies.append(pltpu.make_async_copy(held.at[plane], grad.at[plane], sems.at[plane]))
        copies[-1].start()
    for copy in copies:
        copy.wait()


def line_sums(own, opposite, t_next, t_prev, sums):
    last = PLANES * COMPS
    sums[...] = (own[...] + opposite[...]) + (t_prev[last] + t_next[last])


def all_sums(count, *refs):
    tile = paired_total([ref[...] for ref in refs[:-1]])
    store_weight_grad(refs[-1], tile * (1.0 / count))


def run(kernel, shapes, *operands, scratch=(), in_hbm=(), out_hbm=(), aliases=()):
    def place(in_far):
        space = pltpu.HBM if in_far else pltpu.VMEM
        return pl.BlockSpec(memory_space=space)

    return pl.pallas_call(
        kernel,
        out_shape=[jax.ShapeDtypeStruct(shape, F32) for shape in shapes],
        in_specs=[place(i in in_hbm) for i in range(len(operands))],
        out_specs=[place(i in out_hbm) for i in range(len(shapes))],
        scratch_shapes=list(scratch),
        input_output_aliases=dict(aliases),
        compiler_params=pltpu.CompilerParams(vmem_limit_bytes=32 * 2**20),
    )(*operands)


def shifted(value, axis, offset):
    count = lax.axis_size(axis)
    return lax.ppermute(value, axis, [(i, (i + offset) % count) for i in range(count)])


def z_planes(block):
    if lax.axis_size("gz") == 2:
        return shifted(block, "gz", 1)
    return jnp.concatenate([shifted(block[:1], "gz", -1), shifted(block[1:], "gz", 1)], axis=0)


def partners(value, axes):
    count = 1
    for axis in axes:
        count *= lax.axis_size(axis)
    if count == 4:
        moved = [lax.ppermute(value, axes, [(i, i ^ k) for i in range(4)]) for k in (1, 2, 3)]
        return [value] + moved
    for axis in axes:
        size = lax.axis_size(axis)
        if size & (size - 1):
            value = lax.psum(value, axis)
            continue
        step = 1
        while step < size:
            value = value + lax.ppermute(value, axis, [(i, i ^ step) for i in range(size)])
            step *= 2
    return [value]


def paired_total(values):
    while len(values) > 1:
        values = [a + b for a, b in zip(values[::2], values[1::2])]
    return values[0]


def weight_table(conv_weights):
    out_index, in_index, turn = np.indices((NCH, NCH, NCH))
    forward_pick = ((out_index + turn) % NCH == in_index).astype(np.float32)
    backward_pick = ((in_index + turn) % NCH == out_index).astype(np.float32)
    wide = conv_weights[:, :, :, None]
    forward = jnp.sum(wide * forward_pick[:, :, None, :], axis=1)
    backward = jnp.sum(wide * backward_pick[:, :, None, :], axis=0)
    table = jnp.concatenate(
        [forward.reshape(NCH, TERMS * NCH), backward.reshape(NCH, TERMS * NCH)], axis=1
    )
    return jnp.concatenate([table, table], axis=0)


def local(gauge_links, input_field, conv_weights, loss_weight):
    shape = input_field.shape
    field_in = to_rows(input_field)
    t_next = shifted(field_in, "ta", -1)
    field, links, t_send, z_send = run(
        pack_forward,
        (FIELD,) * 4,
        pltpu.with_memory_space_constraint(field_in, pltpu.HBM),
        pltpu.with_memory_space_constraint(to_rows(gauge_links), pltpu.HBM),
        scratch=[pltpu.SemaphoreType.DMA((2,))],
        in_hbm=(0, 1),
    )
    t_prev = shifted(t_send, "ta", 1)
    z_near = z_planes(z_send)
    weights = weight_table(conv_weights)
    loss = loss_weight.reshape(PLANES, HALF * LANES)
    partial, near = run(near_forward, (FIELD, (5,) + FIELD), field, links, weights)
    out, cot, far, down, up, z_send = run(
        far_forward,
        (FIELD, FIELD, (3,) + FIELD[1:], MESSAGE, MESSAGE, FIELD),
        links,
        weights,
        loss,
        partial,
        t_next,
        t_prev,
        z_near,
    )
    down, up, sums = run(
        weight_partial,
        (MESSAGE, MESSAGE, TILE),
        field,
        cot,
        near,
        far,
        t_prev,
        z_near,
        down,
        up,
        scratch=[pltpu.VMEM((NCH,) + FIELD, F32)],
        aliases=((6, 0), (7, 1)),
    )
    t_next_cot = shifted(down, "ta", -1)
    t_prev_cot = shifted(up, "ta", 1)
    z_near_cot = z_planes(z_send)
    if lax.axis_size("ta") == 4:
        opposite = shifted(sums, "ta", 2)
    else:
        sums = paired_total(partners(sums, ("ta",)))
    out, partial = run(
        near_backward,
        (FIELD, FIELD),
        out,
        links,
        weights,
        cot,
        scratch=[pltpu.SemaphoreType.DMA],
        out_hbm=(0,),
    )
    sums, partial = lax.optimization_barrier((sums, partial))
    if lax.axis_size("ta") == 4:
        (sums,) = run(line_sums, (TILE,), sums, opposite, t_next_cot, t_prev_cot)
    count = loss_weight.size
    for axis in ("ta", "gz", "rep"):
        count = count * lax.axis_size(axis)
    (weight_grad,) = run(
        functools.partial(all_sums, count),
        ((NCH, NCH, TERMS),),
        *partners(sums, ("gz", "rep")),
    )
    (grad,) = run(
        far_backward,
        (FIELD,),
        links,
        weights,
        partial,
        t_next_cot,
        t_prev_cot,
        z_near_cot,
        scratch=[pltpu.VMEM(FIELD, F32), pltpu.SemaphoreType.DMA((PLANES,))],
        out_hbm=(0,),
    )
    return from_rows(out, shape), from_rows(grad, shape), weight_grad


def solution(mesh):
    split = P(("groups", "rep"), "ta", "gz", None, None, None, None, None)
    return jax.shard_map(
        local,
        mesh=mesh,
        in_specs=(split, split, P(), P(("groups", "rep"), "ta", "gz", None)),
        out_specs=(split, split, P("groups", None, None)),
        check_vma=False,
    )
```

```python
import functools

import jax
import jax.numpy as jnp
import numpy as np
from jax import lax
from jax.experimental import pallas as pl
from jax.experimental.pallas import tpu as pltpu
from jax.sharding import PartitionSpec as P

PLANES = 2
NCH = 4
TERMS = 9
COMPS = 18
HALF = 2
ROWS = HALF * NCH
LANES = 128
LX = 16
FIELD = (PLANES, COMPS, ROWS, LANES)
MESSAGE = (PLANES * COMPS + 1, ROWS, LANES)
TILE = (ROWS, LANES)
F32 = jnp.float32


def to_rows(block):
    planes = block.size // (COMPS * ROWS * LANES)
    split = block.reshape(planes, COMPS, NCH, HALF, LANES)
    return split.transpose(0, 1, 3, 2, 4).reshape(planes, COMPS, ROWS, LANES)


def from_rows(rows, shape):
    split = rows.reshape(PLANES, COMPS, HALF, NCH, LANES)
    return split.transpose(0, 1, 3, 2, 4).reshape(shape)


def sublane_index():
    return lax.broadcasted_iota(jnp.int32, (ROWS, LANES), 0)


def lane_index():
    return lax.broadcasted_iota(jnp.int32, (ROWS, LANES), 1)


def pick_rows(value, index):
    return jnp.take_along_axis(value, index, axis=0, mode="promise_in_bounds")


def as_matrix(items):
    return [[[items[p * 9 + r * 3 + c] for c in range(3)] for r in range(3)] for p in range(2)]


def as_items(matrix):
    return [matrix[p][r][c] for p in range(2) for r in range(3) for c in range(3)]


def total(items):
    result = items[0]
    for item in items[1:]:
        result = result + item
    return result


def product(left, right):
    (lr, li), (rr, ri) = left, right
    out = [[], []]
    for r in range(3):
        out[0].append(
            [
                total([lr[r][k] * rr[k][c] for k in range(3)])
                - total([li[r][k] * ri[k][c] for k in range(3)])
                for c in range(3)
            ]
        )
        out[1].append(
            [
                total([lr[r][k] * ri[k][c] for k in range(3)])
                + total([li[r][k] * rr[k][c] for k in range(3)])
                for c in range(3)
            ]
        )
    return out


def product_left_dagger(left, right):
    (lr, li), (rr, ri) = left, right
    out = [[], []]
    for r in range(3):
        out[0].append(
            [
                total([lr[k][r] * rr[k][c] for k in range(3)])
                + total([li[k][r] * ri[k][c] for k in range(3)])
                for c in range(3)
            ]
        )
        out[1].append(
            [
                total([lr[k][r] * ri[k][c] for k in range(3)])
                - total([li[k][r] * rr[k][c] for k in range(3)])
                for c in range(3)
            ]
        )
    return out


def product_right_dagger(left, right):
    (lr, li), (rr, ri) = left, right
    out = [[], []]
    for r in range(3):
        out[0].append(
            [
                total([lr[r][k] * rr[c][k] for k in range(3)])
                + total([li[r][k] * ri[c][k] for k in range(3)])
                for c in range(3)
            ]
        )
        out[1].append(
            [
                total([li[r][k] * rr[c][k] for k in range(3)])
                - total([lr[r][k] * ri[c][k] for k in range(3)])
                for c in range(3)
            ]
        )
    return out


def hop_forward(link, items):
    matrix = as_matrix(items)
    return as_items(product_right_dagger(product(link, matrix), link))


def hop_backward(link, items):
    matrix = as_matrix(items)
    return as_items(product(product_left_dagger(link, matrix), link))


def load_items(ref, plane):
    return [ref[plane, comp] for comp in range(COMPS)]


def load_link(ref, plane, direction):
    index = (sublane_index() & 4) + direction
    return as_matrix([pick_rows(ref[plane, comp], index) for comp in range(COMPS)])


def step_plane(value, direction, offset):
    lane = lane_index()
    if direction == 3:
        inner = lane & (LX - 1)
        if offset > 0:
            return jnp.where(
                inner == LX - 1,
                pltpu.roll(value, LX - 1, axis=1),
                pltpu.roll(value, LANES - 1, axis=1),
            )
        return jnp.where(
            inner == 0,
            pltpu.roll(value, LANES - LX + 1, axis=1),
            pltpu.roll(value, 1, axis=1),
        )
    if offset > 0:
        moved = pltpu.roll(value, LANES - LX, axis=1)
        return jnp.where(lane >= LANES - LX, pltpu.roll(moved, NCH, axis=0), moved)
    moved = pltpu.roll(value, LX, axis=1)
    return jnp.where(lane < LX, pltpu.roll(moved, NCH, axis=0), moved)


def step_items(items, direction, offset):
    return [step_plane(item, direction, offset) for item in items]


def turned(value):
    sub = sublane_index()
    return [value] + [pick_rows(value, (sub & 4) | ((sub + d) & 3)) for d in range(1, NCH)]


def weight_rows(ref, base, term):
    first = base + term * NCH
    return [
        jnp.broadcast_to(ref[:, first + d : first + d + 1], (ROWS, LANES)) for d in range(NCH)
    ]


def mixed_item(weights, turns):
    return total([weights[d] * turns[d] for d in range(NCH)])


def mixed_items(weights, items):
    return [mixed_item(weights, turned(item)) for item in items]


FORWARD = 0
BACKWARD = TERMS * NCH


def near_forward(field, links, weights, partial, terms):
    for plane in range(PLANES):
        items = load_items(field, plane)
        sums = mixed_items(weight_rows(weights, FORWARD, 0), items)

        def add(term, hop, slot):
            mixed = mixed_items(weight_rows(weights, FORWARD, term), hop)
            for comp in range(COMPS):
                terms[slot, plane, comp] = hop[comp]
                sums[comp] = sums[comp] + mixed[comp]

        for direction in (2, 3):
            link = load_link(links, plane, direction)
            slot = 2 * (direction - 2)
            add(
                2 * direction + 1,
                hop_forward(link, step_items(items, direction, 1)),
                slot,
            )
            add(
                2 * direction + 2,
                step_items(hop_backward(link, items), direction, -1),
                slot + 1,
            )
        link = load_link(links, 0, 1)
        other = load_items(field, 1 - plane)
        if plane == 0:
            add(3, hop_forward(link, other), 4)
        else:
            add(4, hop_backward(link, other), 4)
        for comp in range(COMPS):
            partial[plane, comp] = sums[comp]


def store_items(ref, plane, items):
    for comp in range(COMPS):
        ref[plane, comp] = items[comp]


def store_message(ref, plane, items):
    for comp in range(COMPS):
        ref[plane * COMPS + comp] = items[comp]


def load_message(ref, plane):
    return [ref[plane * COMPS + comp] for comp in range(COMPS)]


def pack_forward(field_in, links_in, field, links, t_send, z_send, sems):
    copies = [
        pltpu.make_async_copy(links_in, links, sems.at[0]),
        pltpu.make_async_copy(field_in, field, sems.at[1]),
    ]
    for copy in copies:
        copy.start()
    for copy in copies:
        copy.wait()
    for plane in range(PLANES):
        items = load_items(field, plane)
        store_items(t_send, plane, hop_backward(load_link(links, plane, 0), items))
        if plane == 1:
            items = hop_backward(load_link(links, 1, 1), items)
        store_items(z_send, plane, items)


def early_forward(links, weights, partial, t_next, sums_out, terms):
    for plane in range(PLANES):
        sums = load_items(partial, plane)

        def add(term, hop):
            mixed = mixed_items(weight_rows(weights, FORWARD, term), hop)
            for comp in range(COMPS):
                sums[comp] = sums[comp] + mixed[comp]

        hop = hop_forward(load_link(links, plane, 0), load_items(t_next, plane))
        store_items(terms, plane, hop)
        add(1, hop)
        store_items(sums_out, plane, sums)


def far_forward(
    links, weights, loss, partial, t_prev, z_near, out, cot, term_three, down, up, z_send
):
    for plane in range(PLANES):
        sums = load_items(partial, plane)

        def add(term, hop):
            mixed = mixed_items(weight_rows(weights, FORWARD, term), hop)
            for comp in range(COMPS):
                sums[comp] = sums[comp] + mixed[comp]

        if plane == 0:
            add(4, load_items(z_near, 1))
        else:
            hop = hop_forward(load_link(links, 1, 1), load_items(z_near, 0))
            for comp in range(COMPS):
                term_three[comp] = hop[comp]
            add(3, hop)
        add(2, load_items(t_prev, plane))
        row = loss[plane : plane + 1, :]
        scale = jnp.where(
            sublane_index() < NCH,
            jnp.broadcast_to(row[:, :LANES], (ROWS, LANES)),
            jnp.broadcast_to(row[:, LANES:], (ROWS, LANES)),
        )
        store_items(out, plane, sums)
        cots = [scale * item for item in sums]
        store_items(cot, plane, cots)
        turns = [turned(item) for item in cots]

        def pulled(direction):
            rows = weight_rows(weights, BACKWARD, 2 * direction + 1)
            items = [mixed_item(rows, turn) for turn in turns]
            return hop_backward(load_link(links, plane, direction), items)

        store_message(down, plane, cots)
        store_message(up, plane, pulled(0))
        store_items(z_send, plane, pulled(1) if plane == 1 else cots)


def term_item(sources, term, plane, comp):
    field, near, far, three, t_prev, z_near = sources
    if term == 0:
        return field[plane, comp]
    if term == 1:
        return far[plane, comp]
    if term == 2:
        return t_prev[plane, comp]
    if term >= 5:
        return near[term - 5, plane, comp]
    if (term == 3) == (plane == 0):
        return near[4, plane, comp]
    return three[comp] if term == 3 else z_near[1, comp]


def weight_sums(sources, cot, sums, spread):
    sub = sublane_index()
    lane = lane_index()
    for channel in range(NCH):
        index = (sub & 4) + channel
        for plane in range(PLANES):
            for comp in range(COMPS):
                spread[channel, plane, comp] = pick_rows(cot[plane, comp], index)
    rows = [jnp.zeros((ROWS, LANES), F32) for _ in range(2)]
    for term in range(TERMS):
        parts = [None] * NCH
        for plane in range(PLANES):
            for comp in range(COMPS):
                value = term_item(sources, term, plane, comp)
                for channel in range(NCH):
                    piece = spread[channel, plane, comp] * value
                    parts[channel] = piece if parts[channel] is None else parts[channel] + piece
        for channel in range(NCH):
            summed = jnp.sum(parts[channel], axis=1, keepdims=True)
            place = lane == (channel >> 1) * LX + term
            rows[channel & 1] = jnp.where(place, summed, rows[channel & 1])
    even, odd = [row + pltpu.roll(row, NCH, axis=0) for row in rows]
    sums[...] = jnp.where(sub < NCH, even, odd)


def store_weight_grad(ref, tile):
    for channel in range(NCH):
        moved = pltpu.roll(tile, LANES - LX, axis=1) if channel >> 1 else tile
        first = (channel & 1) * NCH
        ref[channel] = moved[first : first + NCH, :TERMS]


def weight_partial(field, cot, near, far, three, t_prev, z_near, *refs):
    down, up, sums, spread = refs[2:]
    weight_sums((field, near, far, three, t_prev, z_near), cot, sums, spread)
    for ref in (down, up):
        ref[PLANES * COMPS] = sums[...]


def near_backward(out_in, links, weights, cot, out, partial, sem):
    copy = pltpu.make_async_copy(out_in, out, sem)
    copy.start()
    for plane in range(PLANES):
        near_backward_plane(plane, links, weights, cot, partial)
    copy.wait()


def near_backward_plane(plane, links, weights, cot, partial):
    turns = [turned(cot[plane, comp]) for comp in range(COMPS)]

    def mixed(term):
        rows = weight_rows(weights, BACKWARD, term)
        return [mixed_item(rows, turn) for turn in turns]

    grads = mixed(0)

    def add(hop):
        for comp in range(COMPS):
            grads[comp] = grads[comp] + hop[comp]

    for direction in (2, 3):
        link = load_link(links, plane, direction)
        pulled = hop_backward(link, mixed(2 * direction + 1))
        add(step_items(pulled, direction, -1))
        add(hop_forward(link, step_items(mixed(2 * direction + 2), direction, 1)))
    link = load_link(links, 0, 1)
    term = 4 - plane
    other = mixed_items(weight_rows(weights, BACKWARD, term), load_items(cot, 1 - plane))
    add(hop_backward(link, other) if plane == 1 else hop_forward(link, other))
    for comp in range(COMPS):
        partial[plane, comp] = grads[comp]


def far_backward(links, weights, partial, t_next, t_prev, z_near, grad, held, sems):
    copies = []
    for plane in range(PLANES):
        grads = load_items(partial, plane)

        def add(hop):
            for comp in range(COMPS):
                grads[comp] = grads[comp] + hop[comp]

        def pushed(direction, term, items):
            mixed = mixed_items(weight_rows(weights, BACKWARD, term), items)
            return hop_forward(load_link(links, plane, direction), mixed)

        add(pushed(1, 4, load_items(z_near, 0)) if plane == 1 else load_items(z_near, 1))
        add(load_message(t_prev, plane))
        add(pushed(0, 2, load_message(t_next, plane)))
        store_items(held, plane, grads)
        copies.append(pltpu.make_async_copy(held.at[plane], grad.at[plane], sems.at[plane]))
        copies[-1].start()
    for copy in copies:
        copy.wait()


def line_sums(own, opposite, t_next, t_prev, sums):
    last = PLANES * COMPS
    sums[...] = (own[...] + opposite[...]) + (t_prev[last] + t_next[last])


def all_sums(count, *refs):
    tile = paired_total([ref[...] for ref in refs[:-1]])
    store_weight_grad(refs[-1], tile * (1.0 / count))


def run(kernel, shapes, *operands, scratch=(), in_hbm=(), out_hbm=(), aliases=()):
    def place(in_far):
        space = pltpu.HBM if in_far else pltpu.VMEM
        return pl.BlockSpec(memory_space=space)

    return pl.pallas_call(
        kernel,
        out_shape=[jax.ShapeDtypeStruct(shape, F32) for shape in shapes],
        in_specs=[place(i in in_hbm) for i in range(len(operands))],
        out_specs=[place(i in out_hbm) for i in range(len(shapes))],
        scratch_shapes=list(scratch),
        input_output_aliases=dict(aliases),
        compiler_params=pltpu.CompilerParams(vmem_limit_bytes=32 * 2**20),
    )(*operands)


def shifted(value, axis, offset):
    count = lax.axis_size(axis)
    return lax.ppermute(value, axis, [(i, (i + offset) % count) for i in range(count)])


def z_planes(block):
    if lax.axis_size("gz") == 2:
        return shifted(block, "gz", 1)
    return jnp.concatenate([shifted(block[:1], "gz", -1), shifted(block[1:], "gz", 1)], axis=0)


def partners(value, axes):
    count = 1
    for axis in axes:
        count *= lax.axis_size(axis)
    if count == 4:
        moved = [lax.ppermute(value, axes, [(i, i ^ k) for i in range(4)]) for k in (1, 2, 3)]
        return [value] + moved
    for axis in axes:
        size = lax.axis_size(axis)
        if size & (size - 1):
            value = lax.psum(value, axis)
            continue
        step = 1
        while step < size:
            value = value + lax.ppermute(value, axis, [(i, i ^ step) for i in range(size)])
            step *= 2
    return [value]


def paired_total(values):
    while len(values) > 1:
        values = [a + b for a, b in zip(values[::2], values[1::2])]
    return values[0]


def weight_table(conv_weights):
    out_index, in_index, turn = np.indices((NCH, NCH, NCH))
    forward_pick = ((out_index + turn) % NCH == in_index).astype(np.float32)
    backward_pick = ((in_index + turn) % NCH == out_index).astype(np.float32)
    wide = conv_weights[:, :, :, None]
    forward = jnp.sum(wide * forward_pick[:, :, None, :], axis=1)
    backward = jnp.sum(wide * backward_pick[:, :, None, :], axis=0)
    table = jnp.concatenate(
        [forward.reshape(NCH, TERMS * NCH), backward.reshape(NCH, TERMS * NCH)], axis=1
    )
    return jnp.concatenate([table, table], axis=0)


def local(gauge_links, input_field, conv_weights, loss_weight):
    shape = input_field.shape
    field_in = to_rows(input_field)
    t_next = shifted(field_in, "ta", -1)
    field, links, t_send, z_send = run(
        pack_forward,
        (FIELD,) * 4,
        pltpu.with_memory_space_constraint(field_in, pltpu.HBM),
        pltpu.with_memory_space_constraint(to_rows(gauge_links), pltpu.HBM),
        scratch=[pltpu.SemaphoreType.DMA((2,))],
        in_hbm=(0, 1),
    )
    t_prev = shifted(t_send, "ta", 1)
    z_near = z_planes(z_send)
    weights = weight_table(conv_weights)
    loss = loss_weight.reshape(PLANES, HALF * LANES)
    partial, near = run(near_forward, (FIELD, (5,) + FIELD), field, links, weights)
    partial, far = run(
        early_forward,
        (FIELD, FIELD),
        links,
        weights,
        partial,
        t_next,
    )
    out, cot, three, down, up, z_send = run(
        far_forward,
        (FIELD, FIELD, FIELD[1:], MESSAGE, MESSAGE, FIELD),
        links,
        weights,
        loss,
        partial,
        t_prev,
        z_near,
    )
    down, up, sums = run(
        weight_partial,
        (MESSAGE, MESSAGE, TILE),
        field,
        cot,
        near,
        far,
        three,
        t_prev,
        z_near,
        down,
        up,
        scratch=[pltpu.VMEM((NCH,) + FIELD, F32)],
        aliases=((7, 0), (8, 1)),
    )
    t_next_cot = shifted(down, "ta", -1)
    t_prev_cot = shifted(up, "ta", 1)
    z_near_cot = z_planes(z_send)
    if lax.axis_size("ta") == 4:
        opposite = shifted(sums, "ta", 2)
    else:
        sums = paired_total(partners(sums, ("ta",)))
    out, partial = run(
        near_backward,
        (FIELD, FIELD),
        out,
        links,
        weights,
        cot,
        scratch=[pltpu.SemaphoreType.DMA],
        out_hbm=(0,),
    )
    sums, partial = lax.optimization_barrier((sums, partial))
    if lax.axis_size("ta") == 4:
        (sums,) = run(line_sums, (TILE,), sums, opposite, t_next_cot, t_prev_cot)
    count = loss_weight.size
    for axis in ("ta", "gz", "rep"):
        count = count * lax.axis_size(axis)
    (weight_grad,) = run(
        functools.partial(all_sums, count),
        ((NCH, NCH, TERMS),),
        *partners(sums, ("gz", "rep")),
    )
    (grad,) = run(
        far_backward,
        (FIELD,),
        links,
        weights,
        partial,
        t_next_cot,
        t_prev_cot,
        z_near_cot,
        scratch=[pltpu.VMEM(FIELD, F32), pltpu.SemaphoreType.DMA((PLANES,))],
        out_hbm=(0,),
    )
    return from_rows(out, shape), from_rows(grad, shape), weight_grad


def solution(mesh):
    split = P(("groups", "rep"), "ta", "gz", None, None, None, None, None)
    return jax.shard_map(
        local,
        mesh=mesh,
        in_specs=(split, split, P(), P(("groups", "rep"), "ta", "gz", None)),
        out_specs=(split, split, P("groups", None, None)),
        check_vma=False,
    )
```
